32 devices in a mesh: fsdp: 4 (over y, x), context: 4 (over z), tensor: 2 (over core).
Axes of the slice: x: 2, y: 2, z: 4, core: 2. Of those that a mesh axis runs over, the one named last changes fastest.
Arguments:
- tokens: bfloat16 [12288, 768], P(('fsdp', 'context')), may hold values from -6 to 6
- cotangent: bfloat16 [12288, 768], P(('fsdp', 'context')), may hold values from -6 to 6
- w_qkv: bfloat16 [3, 768, 768], P(None, 'fsdp', 'tensor'), may hold values from -0.21875 to 0.21875
- bias_qv: float32 [2, 768], P(None, 'tensor'), may hold values from -3 to 3
- w_attn_out: bfloat16 [768, 768], P('tensor', 'fsdp'), may hold values from -1.25 to 1.25
- w_up: bfloat16 [768, 3072], P('fsdp', 'tensor'), may hold values from -0.21875 to 0.21875
- bias_up: float32 [3072], P('tensor'), may hold values from -3 to 3
- w_down: bfloat16 [3072, 768], P('tensor', 'fsdp'), may hold values from -0.109375 to 0.109375
- gains: float32 [2, 768], replicated, may hold values from 0.1 to 1.9
- shifts: float32 [4, 768], replicated, may hold values from -3 to 3
- seq_lengths: int32 [4, 3], P('fsdp'), may hold values from 1 to 1536, 3072 in all within a row
- key_mask: int32 [12288], P('fsdp'), may hold values 0 or 1
Outputs:
- out: bfloat16 [12288, 768], P(('fsdp', 'context'))
- grad_tokens: bfloat16 [12288, 768], P(('fsdp', 'context'))
- grad_qkv: float32 [3, 768, 768], P(None, 'fsdp', 'tensor')
- grad_attn_out: float32 [768, 768], P('tensor', 'fsdp')
- grad_up: float32 [768, 3072], P('fsdp', 'tensor')
- grad_down: float32 [3072, 768], P('tensor', 'fsdp')
- grad_bias_qv: float32 [2, 768], P(None, 'tensor')
- grad_bias_up: float32 [3072], P('tensor')
- grad_gains: float32 [2, 768], replicated
- grad_shifts: float32 [4, 768], replicated
The draws below stay inside these ranges and needn't reach their ends.
Inputs may be any that keep to these rules, and one draw needn't show every extreme that they name: `seq_lengths`: row f holds the lengths of the 3 sequences packed in order into the 3072 rows of group f; they sum to 3072 and the longest is 1536 in every row. `key_mask`: 1 marks a row that other rows of its sequence attend to; every row attends to itself.
All inputs are finite; a program needn't handle non-finite values. No bound on the sum of `key_mask` on one device may be relied on, other than what follows from the above.
Results may differ from the reference program's by a relative error of at most 0.022.
Values may be sent and summed in bfloat16 or wider, within the bound.
No kernel may reach another device: no remote copies, remote signals or barrier semaphores. Data moves between devices by JAX's collectives and lax.ppermute only.
A program may use at most 192 MiB of HBM per device.

```python
import math
import jax
import jax.numpy as jnp
import numpy as np
from jax import lax

D = 768
H = 12
HD = 64
FF = 3072
TOK_DEV = 768
SEQS = 3
GROUP = 3072
SEQ_MOST = 1536
TOKENS = 12288
N_FSDP = 4
N_CONTEXT = 4


def with_ends(array, key, smallest, top_value):
    longest = array.shape.index(max(array.shape))
    spots = []
    for shift in (0, 1):
        where = [jax.random.randint(jax.random.fold_in(key, axis), (), 0, length) for axis, length in enumerate(array.shape)]
        where[longest] = (where[longest] + shift) % array.shape[longest]
        spots.append(tuple(where))
    return array.at[spots[0]].set(smallest).at[spots[1]].set(top_value)


def raised(drawn, stream_key, source, target, shards_of, factor):
    owner, partner = [(jnp.arange(drawn.shape[position]) // (drawn.shape[position] // shards_of)).reshape([-1 if axis == position else 1 for axis in range(drawn.ndim)]) for position in (source, target)]
    chosen = jax.random.permutation(stream_key, shards_of)[partner]
    strong = (owner == chosen) | (owner == (partner + shards_of // 2) % shards_of)
    return jnp.where(strong, factor * drawn, drawn)


def level_of(stream_key, shape, pieces, least, high):
    level, own = 1.0, jax.random.fold_in(stream_key, 6)
    for dim, parts in pieces:
        draws = jnp.exp(jax.random.uniform(jax.random.fold_in(own, dim), (parts,), jnp.float32, least / len(pieces), high / len(pieces)))
        level = level * jnp.repeat(draws, shape[dim] // parts).reshape([-1 if axis == dim else 1 for axis in range(len(shape))])
    return level


def length_profile(number_of, total, most, skew):
    weights = [(1 << 20) // math.isqrt(standing ** skew) + 1 for standing in range(2, number_of + 1)]
    spare, holding = total - most - (number_of - 1), [1] * (number_of - 1)
    while spare > 0:
        movable = [i for i in range(number_of - 1) if holding[i] < most]
        whole, budget = sum([weights[i] for i in movable]), spare
        for i in movable:
            extra = min(most - holding[i], max(1, budget * weights[i] // whole), spare)
            holding[i] = holding[i] + extra
            spare = spare - extra
    return np.array([most] + holding)


def uneven(rng, amount, total, reach, lean):
    if amount == 2:
        one = jax.random.randint(rng, (), max(1, total - reach), min(reach, total - 1) + 1)
        return jnp.stack([one, total - one])
    tallies = jnp.asarray(length_profile(amount, total, reach, lean), jnp.int32)
    couples = (amount - 1) // 2
    source_of, taker = tallies[1:1 + 2 * couples:2], tallies[2:2 + 2 * couples:2]
    room = jnp.minimum(source_of - 1, reach - taker)
    shifted = jax.random.randint(jax.random.fold_in(rng, 1), (couples,), 0, 1 << 20) % (room + 1)
    tallies = tallies.at[1:1 + 2 * couples:2].set(source_of - shifted).at[2:2 + 2 * couples:2].set(taker + shifted)
    return tallies[jax.random.permutation(jax.random.fold_in(rng, 2), amount)]


def gaussian(rng, extent, scale, bound, shards=(), held_as=jnp.bfloat16):
    entries = scale * jax.random.normal(rng, extent, jnp.float32)
    if shards:
        entries = entries * level_of(rng, extent, shards, -0.22, 0.18)
    return jnp.clip(entries, -bound, bound).astype(held_as)


def bell_draw_with(rng, shape, scale, bound, cuts, heavy, kind=jnp.bfloat16):
    values = scale * jax.random.normal(rng, shape, jnp.float32)
    if cuts:
        values = values * level_of(rng, shape, cuts, -0.22, 0.18)
    return jnp.clip(raised(values, jax.random.fold_in(rng, 3), *heavy), -bound, bound).astype(kind)


def setup_inputs(seed: int = 0) -> dict:
    key_list = jax.random.split(jax.random.key(seed), 13)
    tokens = bell_draw_with(key_list[0], (TOKENS, D), 1.0, 6.0, ((0, 16),), (0, 1, 16, 2.0))
    cotangent = gaussian(key_list[1], (TOKENS, D), 1.0, 6.0, ((0, 16),))
    w_qkv = gaussian(key_list[2], (3, D, D), D ** -0.5, 0.21875, ((1, 4), (2, 2)))
    bias_qv = gaussian(key_list[3], (2, D), 0.5, 3.0, ((1, 2),), jnp.float32)
    w_attn_out = gaussian(key_list[4], (D, D), (D // 32) ** -0.5, 1.25, ((0, 2), (1, 4)))
    w_up = gaussian(key_list[5], (D, FF), D ** -0.5, 0.21875, ((0, 4), (1, 2)))
    bias_up = gaussian(key_list[6], (FF,), 0.5, 3.0, ((0, 2),), jnp.float32)
    w_down = gaussian(key_list[7], (FF, D), FF ** -0.5, 0.109375, ((0, 2), (1, 4)))
    gains = jnp.clip(1.0 + 0.18 * jax.random.normal(key_list[8], (2, D), jnp.float32), 0.1, 1.9)
    shifts = gaussian(key_list[9], (4, D), 0.5, 3.0, (), jnp.float32)
    seq_lengths = jax.vmap(lambda own: uneven(own, SEQS, GROUP, SEQ_MOST, 2))(jax.random.split(key_list[10], N_FSDP)).reshape((N_FSDP, SEQS)).astype(jnp.int32)
    key_mask = with_ends((jax.random.randint(key_list[11], (TOKENS,), 0, 8) < 7).astype(jnp.int32), jax.random.fold_in(key_list[11], 1), 0, 1)
    return {"tokens": tokens, "cotangent": cotangent, "w_qkv": w_qkv, "bias_qv": bias_qv, "w_attn_out": w_attn_out, "w_up": w_up, "bias_up": bias_up, "w_down": w_down, "gains": gains, "shifts": shifts, "seq_lengths": seq_lengths, "key_mask": key_mask}


EPSILON = 1e-12
SCORE_SCALE = 0.125
MASKED_SCORE = -1e+30

@jax.custom_vjp
def low(v):
    return lax.optimization_barrier(v.astype(jnp.bfloat16)).astype(jnp.float32)

@jax.custom_vjp
def low_back(v):
    return v

def low_keep(v):
    return (low(v), None)

def low_pass(kept, grad):
    return (grad,)

def back_keep(v):
    return (v, None)

def back_low(kept, grad):
    return (low(grad),)
low.defvjp(low_keep, low_pass)
low_back.defvjp(back_keep, back_low)

def both_ways(value):
    return low(low_back(value))

def matmul(left, right):
    return jnp.dot(left, right, precision=lax.Precision.HIGHEST)

def layer_norm(inputs, gain, shift):
    center = inputs - lax.optimization_barrier(jnp.mean(inputs, axis=-1, keepdims=True))
    spread = lax.optimization_barrier(jnp.mean(center * center, axis=-1, keepdims=True))
    return center * lax.rsqrt(spread + EPSILON) * gain + shift

def segment_ids(lengths_row, places):
    bounds = jnp.cumsum(lengths_row)
    return lax.optimization_barrier(jnp.sum((places[:, None] >= bounds[None, :-1]).astype(jnp.int32), axis=1))

def attention(query, keys, values, segment, places, visible_key):
    total_rows = query.shape[0]
    block_rows = 512 if total_rows % 512 == 0 else total_rows
    blocks = total_rows // block_rows
    key_heads = keys.reshape(total_rows, H, HD)
    value_heads = values.reshape(total_rows, H, HD)

    def one_block(inputs):
        query_block, segment_block, place_block = inputs
        scores = jnp.einsum('qhd,khd->hqk', query_block, key_heads, precision=lax.Precision.HIGHEST) * SCORE_SCALE
        scores = low_back(scores)
        allowed = (segment_block[:, None] == segment[None, :]) & ((visible_key[None, :] == 1) | (place_block[:, None] == places[None, :]))
        masked = jnp.where(allowed[None], scores, MASKED_SCORE)
        row_peak = lax.optimization_barrier(jnp.max(masked, axis=-1, keepdims=True))
        exponent = jnp.where(allowed[None], jnp.exp(masked - row_peak), 0.0)
        softmax_weights = low(exponent / lax.optimization_barrier(jnp.sum(exponent, axis=-1, keepdims=True)))
        result = jnp.einsum('hqk,khd->qhd', softmax_weights, value_heads, precision=lax.Precision.HIGHEST)
        return result.reshape(block_rows, H * HD)
    outputs = lax.map(jax.checkpoint(one_block), (query.reshape(blocks, block_rows, H, HD), segment.reshape(blocks, block_rows), places.reshape(blocks, block_rows)))
    return outputs.reshape(total_rows, H * HD)

def forward(tokens, w_qkv, bias_qv, w_attn_out, w_up, bias_up, w_down, gains, shifts, segment, places, visible_key):
    query = both_ways(matmul(tokens, w_qkv[0]) + bias_qv[0])
    keys = both_ways(matmul(tokens, w_qkv[1]))
    values = both_ways(matmul(tokens, w_qkv[2]) + bias_qv[1])
    attended = both_ways(attention(query, keys, values, segment, places, visible_key))
    branch = low_back(matmul(attended, w_attn_out))
    first = layer_norm(tokens + branch + shifts[0], gains[0], shifts[1])
    first_low = low(first)
    upper = low_back(matmul(first_low, w_up) + bias_up)
    active = low(jax.nn.gelu(upper, approximate=False))
    second = low_back(matmul(active, w_down))
    return layer_norm(first + second + shifts[2], gains[1], shifts[3])

def reference(tokens, cotangent, w_qkv, bias_qv, w_attn_out, w_up, bias_up, w_down, gains, shifts, seq_lengths, key_mask):
    group_rows = TOK_DEV * N_CONTEXT
    weights = (w_qkv.astype(jnp.float32), bias_qv, w_attn_out.astype(jnp.float32), w_up.astype(jnp.float32), bias_up, w_down.astype(jnp.float32), gains, shifts)
    token_groups = tokens.astype(jnp.float32).reshape(N_FSDP, group_rows, D)
    cotangent_groups = cotangent.astype(jnp.float32).reshape(N_FSDP, group_rows, D)
    mask_groups = key_mask.reshape(N_FSDP, group_rows)
    places = jnp.arange(group_rows, dtype=jnp.int32)

    def one_group(carry, inputs):
        group_tokens, group_cotangent, lengths_row, visible_key = inputs
        segment = segment_ids(lengths_row, places)

        def run(group_in, w_proj, b_proj, w_back, w_upper, b_upper, w_lower, gain_rows, shift_rows):
            return forward(group_in, w_proj, b_proj, w_back, w_upper, b_upper, w_lower, gain_rows, shift_rows, segment, places, visible_key)
        result, pullback = jax.vjp(run, group_tokens, weights[0], weights[1], weights[2], weights[3], weights[4], weights[5], weights[6], weights[7])
        grads = pullback(group_cotangent)
        carry = jax.tree.map(lambda running, addend: running + addend, carry, tuple(grads[1:]))
        return (carry, (result, grads[0]))
    zeros = jax.tree.map(jnp.zeros_like, weights)
    totals, (results, input_grads) = lax.scan(one_group, zeros, (token_groups, cotangent_groups, seq_lengths, mask_groups))
    return (results.reshape(TOKENS, D).astype(jnp.bfloat16), input_grads.reshape(TOKENS, D).astype(jnp.bfloat16), totals[0], totals[2], totals[3], totals[5], totals[1], totals[4], totals[6], totals[7])
```

```python
import jax
import jax.numpy as jnp
import numpy as np
from jax import lax
from jax.experimental import pallas as pl
from jax.experimental.pallas import tpu as pltpu
from jax.sharding import PartitionSpec as P

EPSILON = 1e-12
LOG2E = 1.4426950408889634
NEG = -1e30
BQ = 256
BK = 256
F32 = jnp.float32
BF16 = jnp.bfloat16
ROW = (((1,), (1,)), ((), ()))
COL = (((1,), (0,)), ((), ()))
LIMIT = 56 * 1024 * 1024
COST = pl.CostEstimate(flops=36_000_000_000, transcendentals=0, bytes_accessed=8_000_000)
PAIR_COST = pl.CostEstimate(flops=14_000_000_000, transcendentals=0, bytes_accessed=4_000_000)


def dot(a, b, dims=COL):
    return lax.dot_general(a, b, dims, preferred_element_type=F32)


def normalize(inputs):
    center = inputs - jnp.mean(inputs, axis=-1, keepdims=True)
    factor = lax.rsqrt(jnp.mean(center * center, axis=-1, keepdims=True) + EPSILON)
    return (center * factor, factor)


def norm_back(upstream, normed, factor, gain):
    scaled = upstream * gain
    return factor * (
        scaled
        - jnp.mean(scaled, axis=-1, keepdims=True)
        - normed * jnp.mean(scaled * normed, axis=-1, keepdims=True)
    )


def segment_of(places, b1, b2):
    return (places >= b1).astype(jnp.int32) + (places >= b2).astype(jnp.int32)


def key_range(first, last, b1, b2, total):
    lo = jnp.where(first >= b2, b2, jnp.where(first >= b1, b1, 0))
    hi = jnp.where(last >= b2, total, jnp.where(last >= b1, b2, b1))
    return lo, hi


def half_mask(rows, side):
    lane = lax.broadcasted_iota(jnp.int32, (rows, 128), 1)
    return (lane < 64) if side == 0 else (lane >= 64)


def pick(pair, side):
    return jnp.where(half_mask(pair.shape[0], side), pair, jnp.zeros_like(pair))


def fill_bias(bias_ref, kb_ref, first, b1, b2, j0, j1):
    rows = first + lax.broadcasted_iota(jnp.int32, (BQ, 1), 0)
    row_seg = segment_of(rows, b1, b2)

    def body(j, carry):
        cols = j * BK + lax.broadcasted_iota(jnp.int32, (1, BK), 1)
        col_seg = segment_of(cols, b1, b2)
        kept = jnp.where(rows == cols, 0.0, jnp.broadcast_to(kb_ref[j], (BQ, BK)))
        bias_ref[j] = jnp.where(row_seg == col_seg, kept, NEG)
        return carry

    lax.fori_loop(j0, j1, body, 0)


def attend_kernel(s_ref, q_ref, k_ref, v_ref, kb_ref, o_ref, lse_ref, lset_ref, score, bias):
    total = k_ref.shape[0]
    pairs = q_ref.shape[1] // 128
    b1, b2 = s_ref[0], s_ref[1]
    first = s_ref[2] + pl.program_id(0) * BQ
    lo, hi = key_range(first, first + BQ - 1, b1, b2, total)
    j0, j1 = lo // BK, (hi + BK - 1) // BK
    fill_bias(bias, kb_ref, first, b1, b2, j0, j1)
    lane = lax.broadcasted_iota(jnp.int32, (BQ, 128), 1)
    lse_all = jnp.zeros((BQ, 128), F32)
    heads = 2 * pairs
    peak = None
    held = None
    for h in range(-1, heads):
        nxt = h + 1
        if nxt < heads:
            np_, ns = nxt // 2, nxt % 2
            q_head = pick(q_ref[:, np_ * 128 : np_ * 128 + 128], ns)
        if h >= 0:
            cp = h // 2

        def body(j, carry):
            top, tot, acc = carry
            rows = pl.ds(pl.multiple_of(j * BK, BK), BK)
            if nxt < heads:
                s = dot(q_head, k_ref[rows, np_ * 128 : np_ * 128 + 128], ROW) + bias[j]
                score[nxt % 2, j] = s
                top = jnp.maximum(top, jnp.maximum(s[:, :128], s[:, 128:]))
            if h >= 0:
                p = jnp.exp2(score[h % 2, j] - peak)
                tot = tot + (p[:, :128] + p[:, 128:])
                acc = acc + dot(p.astype(BF16), v_ref[rows, cp * 128 : cp * 128 + 128])
            return (top, tot, acc)

        start = (jnp.full((BQ, 128), NEG, F32), jnp.zeros((BQ, 128), F32), jnp.zeros((BQ, 128), F32))
        top, tot, acc = lax.fori_loop(j0, j1, body, start)
        if h >= 0:
            whole = jnp.sum(tot, axis=1, keepdims=True)
            result = acc / whole
            lse_all = jnp.where(lane == h, peak + jnp.log2(whole), lse_all)
            if h % 2 == 0:
                held = result
            else:
                o_ref[:, cp * 128 : cp * 128 + 128] = jnp.where(lane < 64, held, result).astype(BF16)
        peak = jnp.max(top, axis=1, keepdims=True)
    lse_ref[...] = lse_all
    lset_ref[...] = jnp.transpose(lse_all)[: lset_ref.shape[0], :]


def attend(scalars, qkv, kb, rows, pairs):
    total = qkv.shape[0]
    width = pairs * 128
    return pl.pallas_call(
        attend_kernel,
        grid_spec=pltpu.PrefetchScalarGridSpec(
            num_scalar_prefetch=1,
            grid=(rows // BQ,),
            in_specs=[
                pl.BlockSpec((BQ, width), lambda i, s: (s[2] // BQ + i, 0)),
                pl.BlockSpec((total, width), lambda i, s: (0, 1), pipeline_mode=pl.Buffered(1)),
                pl.BlockSpec((total, width), lambda i, s: (0, 2), pipeline_mode=pl.Buffered(1)),
                pl.BlockSpec((total // BK, 1, BK), lambda i, s: (0, 0, 0)),
            ],
            out_specs=[
                pl.BlockSpec((BQ, width), lambda i, s: (i, 0)),
                pl.BlockSpec((BQ, 128), lambda i, s: (i, 0)),
                pl.BlockSpec((8, BQ), lambda i, s: (0, i)),
            ],
            scratch_shapes=[
                pltpu.VMEM((2, total // BK, BQ, BK), F32),
                pltpu.VMEM((total // BK, BQ, BK), F32),
            ],
        ),
        out_shape=[
            jax.ShapeDtypeStruct((rows, width), BF16),
            jax.ShapeDtypeStruct((rows, 128), F32),
            jax.ShapeDtypeStruct((8, rows), F32),
        ],
        compiler_params=pltpu.CompilerParams(
            dimension_semantics=("arbitrary",), vmem_limit_bytes=LIMIT
        ),
        cost_estimate=COST,
        name="attend",
    )(scalars, qkv, qkv, qkv, kb)


def query_kernel(s_ref, q_ref, k_ref, v_ref, do_ref, o_ref, lse_ref, kb_ref, dq_ref, bias):
    total = k_ref.shape[0]
    pairs = q_ref.shape[1] // 128
    b1, b2 = s_ref[0], s_ref[1]
    first = s_ref[2] + pl.program_id(0) * BQ
    lo, hi = key_range(first, first + BQ - 1, b1, b2, total)
    j0, j1 = lo // BK, (hi + BK - 1) // BK
    fill_bias(bias, kb_ref, first, b1, b2, j0, j1)
    low = half_mask(BQ, 0)
    for p in range(pairs):
        span = slice(p * 128, p * 128 + 128)
        grads = do_ref[:, span]
        product = grads.astype(F32) * o_ref[:, span].astype(F32)
        sides = []
        for side in range(2):
            h = 2 * p + side
            sides.append(
                (
                    pick(q_ref[:, span], side),
                    pick(grads, side),
                    jnp.sum(pick(product, side), axis=1, keepdims=True),
                    lse_ref[:, h : h + 1],
                )
            )

        def body(j, accs):
            rows = pl.ds(pl.multiple_of(j * BK, BK), BK)
            keys = k_ref[rows, span]
            values = v_ref[rows, span]
            out = []
            for (qh, gh, delta, lse), acc in zip(sides, accs):
                prob = jnp.exp2(dot(qh, keys, ROW) + bias[j] - lse)
                score = (prob * (dot(gh, values, ROW) - delta)).astype(BF16)
                out.append(acc + dot(score, keys))
            return tuple(out)

        zero = jnp.zeros((BQ, 128), F32)
        left, right = lax.fori_loop(j0, j1, body, (zero, zero))
        dq_ref[:, span] = (jnp.where(low, left, right) * 0.125).astype(BF16)


def query_grads(scalars, qkv, dout, att, lse, kb, rows, pairs):
    total = qkv.shape[0]
    width = pairs * 128
    return pl.pallas_call(
        query_kernel,
        grid_spec=pltpu.PrefetchScalarGridSpec(
            num_scalar_prefetch=1,
            grid=(rows // BQ,),
            in_specs=[
                pl.BlockSpec((BQ, width), lambda i, s: (s[2] // BQ + i, 0)),
                pl.BlockSpec((total, width), lambda i, s: (0, 1), pipeline_mode=pl.Buffered(1)),
                pl.BlockSpec((total, width), lambda i, s: (0, 2), pipeline_mode=pl.Buffered(1)),
                pl.BlockSpec((BQ, width), lambda i, s: (i, 0)),
                pl.BlockSpec((BQ, width), lambda i, s: (i, 0)),
                pl.BlockSpec((BQ, 128), lambda i, s: (i, 0)),
                pl.BlockSpec((total // BK, 1, BK), lambda i, s: (0, 0, 0)),
            ],
            out_specs=pl.BlockSpec((BQ, width), lambda i, s: (i, 0)),
            scratch_shapes=[pltpu.VMEM((total // BK, BQ, BK), F32)],
        ),
        out_shape=jax.ShapeDtypeStruct((rows, width), BF16),
        compiler_params=pltpu.CompilerParams(
            dimension_semantics=("arbitrary",), vmem_limit_bytes=LIMIT
        ),
        cost_estimate=COST,
        name="query_grads",
    )(scalars, qkv, qkv, qkv, dout, att, lse, kb)


def key_kernel(s_ref, k_ref, v_ref, q_ref, do_ref, stat_ref, mask_ref, dk_ref, dv_ref, *, pair, per):
    total = q_ref.shape[0]
    b1, b2 = s_ref[0], s_ref[1]
    first = s_ref[2] + pl.program_id(0) * BK
    lo, hi = key_range(first, first + BK - 1, b1, b2, total)
    j0, j1 = lo // BQ, (hi + BQ - 1) // BQ
    rows = first + lax.broadcasted_iota(jnp.int32, (BK, 1), 0)
    row_seg = segment_of(rows, b1, b2)
    masked = jnp.transpose(jnp.broadcast_to(mask_ref[0], (128, BK)))[:, :1]
    sides = [(pick(k_ref[...], side), pick(v_ref[...], side)) for side in range(2)]

    def body(j, carry):
        span = pl.ds(pl.multiple_of(j * BQ, BQ), BQ)
        cols = j * BQ + lax.broadcasted_iota(jnp.int32, (1, BQ), 1)
        col_seg = segment_of(cols, b1, b2)
        bias = jnp.where(row_seg == col_seg, jnp.where(rows == cols, 0.0, masked), NEG)
        queries = q_ref[span, :]
        grads = do_ref[span, :]
        place = ((j // per) ^ s_ref[3]) * per + lax.rem(j, per)
        spot = pl.ds(pl.multiple_of(place * BQ, BQ), BQ)
        out = []
        for side in range(2):
            h = 2 * pair + side
            kh, vh = sides[side]
            dk, dv = carry[2 * side], carry[2 * side + 1]
            prob = jnp.exp2(dot(kh, queries, ROW) + bias - stat_ref[h : h + 1, spot])
            score = prob * (dot(vh, grads, ROW) - stat_ref[8 + h : 9 + h, spot])
            out.append(dk + dot(score.astype(BF16), queries))
            out.append(dv + dot(prob.astype(BF16), grads))
        return tuple(out)

    zero = jnp.zeros((BK, 128), F32)
    k0, v0, k1, v1 = lax.fori_loop(j0, j1, body, (zero, zero, zero, zero))
    low = half_mask(BK, 0)
    dk_ref[...] = (jnp.where(low, k0, k1) * (1.0 / LOG2E)).astype(BF16)
    dv_ref[...] = jnp.where(low, v0, v1).astype(BF16)


def key_grads(scalars, qkv, dout, stats, kb, rows, pairs, pair):
    total = qkv.shape[0]

    def kernel(*refs):
        key_kernel(*refs, pair=pair, per=rows // BQ)

    return pl.pallas_call(
        kernel,
        grid_spec=pltpu.PrefetchScalarGridSpec(
            num_scalar_prefetch=1,
            grid=(rows // BK,),
            in_specs=[
                pl.BlockSpec((BK, 128), lambda i, s: (s[2] // BK + i, pairs + pair)),
                pl.BlockSpec((BK, 128), lambda i, s: (s[2] // BK + i, 2 * pairs + pair)),
                pl.BlockSpec((total, 128), lambda i, s: (0, pair), pipeline_mode=pl.Buffered(1)),
                pl.BlockSpec((total, 128), lambda i, s: (0, pair), pipeline_mode=pl.Buffered(1)),
                pl.BlockSpec((16, total), lambda i, s: (0, 0), pipeline_mode=pl.Buffered(1)),
                pl.BlockSpec((1, 1, BK), lambda i, s: (s[2] // BK + i, 0, 0)),
            ],
            out_specs=[
                pl.BlockSpec((BK, 128), lambda i, s: (i, 0)),
                pl.BlockSpec((BK, 128), lambda i, s: (i, 0)),
            ],
        ),
        out_shape=[jax.ShapeDtypeStruct((rows, 128), BF16)] * 2,
        compiler_params=pltpu.CompilerParams(
            dimension_semantics=("arbitrary",), vmem_limit_bytes=LIMIT
        ),
        cost_estimate=PAIR_COST,
        name="key_grads",
    )(scalars, qkv, qkv, qkv, dout, stats, kb)


def place(scalars, pieces, spots, total, cuts):
    count = len(pieces)

    def kernel(s_ref, *refs):
        ins, outs, sem = refs[:count], refs[count:-1], refs[-1]
        copies = []
        for i in range(count):
            height, start = spots[i](s_ref)
            unit = 192 if height % 192 == 0 else 16
            for k, (low, wide) in enumerate(cuts):
                copies.append(
                    pltpu.make_async_copy(
                        ins[i].at[pl.ds(0, height), pl.ds(low, wide)],
                        outs[k].at[pl.ds(pl.multiple_of(start, unit), height), :],
                        sem.at[i * len(cuts) + k],
                    )
                )
        for copy in copies:
            copy.start()
        for copy in copies:
            copy.wait()

    return pl.pallas_call(
        kernel,
        grid_spec=pltpu.PrefetchScalarGridSpec(
            num_scalar_prefetch=1,
            grid=(1,),
            in_specs=[pl.BlockSpec(memory_space=pl.ANY)] * count,
            out_specs=[pl.BlockSpec(memory_space=pl.ANY)] * len(cuts),
            scratch_shapes=[pltpu.SemaphoreType.DMA((count * len(cuts),))],
        ),
        out_shape=[jax.ShapeDtypeStruct((total, wide), BF16) for _, wide in cuts],
        name="place",
    )(scalars, *pieces)


def split(value):
    high = lax.reduce_precision(value, 8, 7)
    return high.astype(BF16), (value - high).astype(BF16)


def after(value, *others):
    return lax.optimization_barrier((value, others))[0]


def solution(mesh):
    n_fsdp, n_context = mesh.shape["fsdp"], mesh.shape["context"]
    direct_f, direct_c = n_fsdp == 4, n_context == 4
    swap = [(0, 1), (1, 0)]

    def partner(value, axis, d):
        return lax.ppermute(value, axis, [(i, i ^ d) for i in range(4)])

    def twin(value):
        return lax.ppermute(value, "tensor", swap)

    def pair_sum(value):
        low = value.astype(BF16)
        return low.astype(F32) + twin(low).astype(F32)

    def gather_weight(scalars, shard, cuts):
        if not direct_f:
            whole = lax.all_gather(shard, "fsdp", axis=0, tiled=True)
            return [whole[:, low : low + wide] for low, wide in cuts]
        rows = shard.shape[0]
        pieces = [shard] + [partner(shard, "fsdp", d) for d in (1, 2, 3)]
        spots = [lambda s, d=d: (rows, (s[6] ^ d) * rows) for d in range(4)]
        return place(scalars, pieces, spots, 4 * rows, cuts)

    def gather_rows(scalars, block, stats=None):
        if not direct_c:
            whole = lax.all_gather(block, "context", axis=0, tiled=True)
            if stats is None:
                return whole, None
            return whole, lax.all_gather(stats, "context", axis=1, tiled=True)
        core, rows = lax.axis_index("tensor"), block.shape[0]
        half = rows // 2
        mine = lax.dynamic_slice_in_dim(block, core * half, half, 0)
        if stats is not None:
            mine = jnp.concatenate((mine,) + split(stats), axis=0)
            near = partner(mine, "context", 1)
            inner = lax.ppermute(mine, "context", [(1, 2), (2, 1)])
            far = partner(mine, "context", 2)
        else:
            near = partner(mine, "context", 1)
            inner = lax.ppermute(mine, "context", [(1, 2), (2, 1)])
            far = lax.ppermute(near, "context", [(1, 2), (2, 1)]) + lax.ppermute(
                inner, "context", [(1, 0), (2, 3)]
            )
        pieces = [block]
        spots = [lambda s: (rows, s[4] * rows)]
        for d, got in ((1, near), (2, far), (3, inner)):
            pieces.append(got)
            spots.append(lambda s, d=d: (half, (s[4] ^ d) * rows + s[5] * half))
            pieces.append(twin(got))
            spots.append(lambda s, d=d: (half, (s[4] ^ d) * rows + (1 - s[5]) * half))
        whole = place(scalars, pieces, spots, 4 * rows, [(0, block.shape[1])])[0]
        if stats is None:
            return whole, None
        high = [got[half : half + 16].astype(F32) for got in (near, far, inner)]
        low = [got[half + 16 :].astype(F32) for got in (near, far, inner)]
        return whole, jnp.concatenate([stats] + [a + b for a, b in zip(high, low)], axis=1)

    def pack(small, cols):
        high, low = split(small)
        filler = jnp.zeros((16 - 2 * small.shape[0], cols), BF16)
        return jnp.concatenate([high, low, filler], axis=0)

    def unpack(block, rows):
        return block[:rows].astype(F32) + block[rows : 2 * rows].astype(F32)

    def stage_f(partial, small=None):
        if not direct_f:
            share = lax.psum_scatter(partial, "fsdp", scatter_dimension=0, tiled=True)
            return share, None if small is None else lax.psum(small, "fsdp")
        me, rows, cols = lax.axis_index("fsdp"), partial.shape[0] // 4, partial.shape[1]
        pieces = [lax.dynamic_slice_in_dim(partial, (me ^ d) * rows, rows, 0) for d in range(4)]
        if small is None:
            got = [partner(pieces[d], "fsdp", d) for d in (1, 2, 3)]
        else:
            extra = pack(small, cols)
            got = [
                partner(jnp.concatenate([pieces[d], extra], axis=0), "fsdp", d) for d in (1, 2, 3)
            ]
        parts = [pieces[0]] + [block[:rows] for block in got]
        parts = [part.astype(F32) for part in parts]
        share = ((parts[0] + parts[1]) + (parts[2] + parts[3])).astype(BF16)
        if small is None:
            return share, None
        more = [unpack(block[rows:], small.shape[0]) for block in got]
        return share, (small + more[0]) + (more[1] + more[2])

    def stage_1(share, small=None):
        if not direct_c:
            return share, small
        side, rows = lax.rem(lax.axis_index("context"), 2), share.shape[0] // 2
        mine = lax.dynamic_slice_in_dim(share, side * rows, rows, 0)
        theirs = lax.dynamic_slice_in_dim(share, (1 - side) * rows, rows, 0)
        return exchange(mine, theirs, small, 1)

    def exchange(mine, theirs, small, d):
        rows = mine.shape[0]
        if small is not None:
            theirs = jnp.concatenate([theirs, pack(small, mine.shape[1])], axis=0)
        got = partner(theirs, "context", d)
        total = (mine.astype(F32) + got[:rows].astype(F32)).astype(BF16)
        if small is not None:
            small = small + unpack(got[rows:], small.shape[0])
        return total, small

    def stage_2(share, small=None):
        if not direct_c:
            return share, small
        return exchange(share, share, small, 2)

    def stage_3(share, small=None):
        if not direct_c:
            total = lax.psum(share, "context").astype(F32)
            return total, None if small is None else lax.psum(small, "context")
        side = lax.rem(lax.axis_index("context"), 2)
        other = partner(share, "context", 1)
        first = jnp.where(side == 0, share, other)
        second = jnp.where(side == 0, other, share)
        return jnp.concatenate([first, second], axis=0).astype(F32), small

    def shards(
        tokens,
        cotangent,
        w_qkv,
        bias_qv,
        w_attn_out,
        w_up,
        bias_up,
        w_down,
        gains,
        shifts,
        seq_lengths,
        key_mask,
    ):
        rows = tokens.shape[0]
        width = w_qkv.shape[2]
        pairs = width // 128
        hidden = w_up.shape[1]
        total = key_mask.shape[0]
        dim = tokens.shape[1]
        b1 = seq_lengths[0, 0]
        b2 = b1 + seq_lengths[0, 1]
        me = lax.axis_index("context")
        order = me if direct_c else 0 * me
        scalars = jnp.stack(
            [b1, b2, me * rows, order, me, lax.axis_index("tensor"), lax.axis_index("fsdp")]
        ).astype(jnp.int32)
        kb = jnp.where(key_mask == 1, 0.0, NEG).astype(F32).reshape(total // BK, 1, BK)

        everyone, _ = gather_rows(scalars, tokens)
        shard = jnp.concatenate([w_qkv[0], w_qkv[1], w_qkv[2]], axis=1)
        (w_proj,) = gather_weight(scalars, shard, [(0, 3 * width)])
        shard = jnp.concatenate([w_attn_out.T, w_up, w_down.T], axis=1)
        shard = after(shard, w_proj)
        cuts = [(0, width), (width, hidden), (width + hidden, hidden)]
        zero = jnp.zeros((width,), F32)
        bias_row = jnp.concatenate([bias_qv[0], zero, bias_qv[1]])
        scale_row = jnp.concatenate([zero + 0.125 * LOG2E, zero + 1.0, zero + 1.0])
        qkv = ((dot(everyone, w_proj) + bias_row) * scale_row).astype(BF16)
        w_back, w_upper, w_lower = gather_weight(scalars, shard, cuts)
        attended, lse, lset = attend(scalars, qkv, kb, rows, pairs)

        branch = pair_sum(dot(attended, w_back, ROW))
        first_sum = tokens.astype(F32) + branch + shifts[0]
        normed1, factor1 = normalize(first_sum)
        first = normed1 * gains[0] + shifts[1]
        first_low = first.astype(BF16)
        upper = dot(first_low, w_upper) + bias_up
        active_f, gelu_back = jax.vjp(lambda values: jax.nn.gelu(values, approximate=False), upper)
        active = active_f.astype(BF16)
        second_sum = first + pair_sum(dot(active, w_lower, ROW)) + shifts[2]
        normed2, factor2 = normalize(second_sum)
        out = (normed2 * gains[1] + shifts[3]).astype(BF16)
        upstream = cotangent.astype(F32)
        gain_two = jnp.sum(upstream * normed2, axis=0)
        shift_three = jnp.sum(upstream, axis=0)
        grad_second = norm_back(upstream, normed2, factor2, gains[1])
        shift_two = jnp.sum(grad_second, axis=0)
        lower_grad = grad_second.astype(BF16)
        group_a, _ = stage_f(dot(lower_grad.T, active).astype(BF16))
        grad_active = dot(lower_grad, w_lower)
        grad_upper = gelu_back(grad_active)[0].astype(BF16)
        grad_bias_up = jnp.sum(grad_upper.astype(F32), axis=0)
        grad_first = grad_second + pair_sum(dot(grad_upper, w_upper, ROW))
        gain_one = jnp.sum(grad_first * normed1, axis=0)
        shift_one = jnp.sum(grad_first, axis=0)
        grad_first_sum = norm_back(grad_first, normed1, factor1, gains[0])
        shift_zero = jnp.sum(grad_first_sum, axis=0)
        branch_grad = grad_first_sum.astype(BF16)

        dout = dot(branch_grad, w_back).astype(BF16)
        marks = np.zeros((8, width), np.float32)
        for h in range(width // 64):
            marks[h, h * 64 : h * 64 + 64] = 1.0
        product = dout.astype(F32) * attended.astype(F32)
        deltat = lax.dot_general(
            jnp.asarray(marks), product, ROW, precision=lax.Precision.HIGHEST,
            preferred_element_type=F32,
        )
        branch_all, stats = gather_rows(scalars, branch_grad, jnp.concatenate([lset, deltat], axis=0))
        group_b, _ = stage_f(
            jnp.concatenate(
                [
                    dot(first_low.T, grad_upper).astype(BF16),
                    dot(branch_grad.T, attended).astype(BF16),
                ],
                axis=1,
            )
        )
        dq = query_grads(scalars, qkv, dout, attended, lse, kb, rows, pairs)
        dout_all = dot(after(branch_all, dq), w_back).astype(BF16)
        group_a, _ = stage_1(after(group_a, dq))
        group_b, _ = stage_1(after(group_b, dq))
        dk0, dv0 = key_grads(scalars, qkv, dout_all, stats, kb, rows, pairs, 0)
        dks, dvs = [dk0], [dv0]
        for pair in range(1, pairs):
            if pair == 1:
                group_a, _ = stage_2(after(group_a, dks[-1]))
                group_b, _ = stage_2(after(group_b, dks[-1]))
            elif pair == 2:
                group_a, _ = stage_3(after(group_a, dks[-1]))
                group_b, _ = stage_3(after(group_b, dks[-1]))
            dk, dv = key_grads(
                after(scalars, dks[-1]), qkv, dout_all, stats, kb, rows, pairs, pair
            )
            dks.append(dk)
            dvs.append(dv)
        if pairs < 3:
            group_a, _ = stage_3(group_a)
            group_b, _ = stage_3(group_b)
        stacked = jnp.concatenate([dq] + dks + dvs, axis=1)
        sums = jnp.sum(stacked.astype(F32), axis=0).reshape(3, width)
        small = jnp.concatenate(
            [gain_one, gain_two, shift_zero, shift_one, shift_two, shift_three, grad_bias_up, sums[0], sums[2]]
        ).reshape(-1, 3 * width)
        group_c, small = stage_f(dot(tokens.T, stacked).astype(BF16), small)
        input_part = pair_sum(dot(stacked, w_proj, ROW))
        grad_tokens = (grad_first_sum + input_part).astype(BF16)
        group_c, small = stage_1(group_c, small)
        group_c, small = stage_2(group_c, small)
        group_c, small = stage_3(group_c, small)
        small = small.reshape(-1)
        sum_gains = small[: 2 * dim].reshape(2, dim)
        sum_shifts = small[2 * dim : 6 * dim].reshape(4, dim)
        sum_bias_up = small[6 * dim : 6 * dim + hidden]
        sum_bias_qv = small[6 * dim + hidden :].reshape(2, width)
        share_qkv = jnp.stack([group_c[:, i * width : (i + 1) * width] for i in range(3)])
        share_lower = group_a.T
        share_upper = group_b[:, :hidden]
        share_back = group_b[:, hidden:].T
        return (
            out,
            grad_tokens,
            share_qkv,
            share_back,
            share_upper,
            share_lower,
            sum_bias_qv,
            sum_bias_up,
            sum_gains,
            sum_shifts,
        )

    return jax.shard_map(
        shards,
        mesh=mesh,
        in_specs=(
            P(("fsdp", "context"), None),
            P(("fsdp", "context"), None),
            P(None, "fsdp", "tensor"),
            P(None, "tensor"),
            P("tensor", "fsdp"),
            P("fsdp", "tensor"),
            P("tensor"),
            P("tensor", "fsdp"),
            P(),
            P(),
            P("fsdp", None),
            P("fsdp"),
        ),
        out_specs=(
            P(("fsdp", "context"), None),
            P(("fsdp", "context"), None),
            P(None, "fsdp", "tensor"),
            P("tensor", "fsdp"),
            P("fsdp", "tensor"),
            P("tensor", "fsdp"),
            P(None, "tensor"),
            P("tensor"),
            P(),
            P(),
        ),
        check_vma=False,
    )
```

```python
import jax
import jax.numpy as jnp
import numpy as np
from jax import lax
from jax.experimental import pallas as pl
from jax.experimental.pallas import tpu as pltpu
from jax.sharding import PartitionSpec as P

EPSILON = 1e-12
LOG2E = 1.4426950408889634
NEG = -1e30
BQ = 256
BK = 256
F32 = jnp.float32
BF16 = jnp.bfloat16
ROW = (((1,), (1,)), ((), ()))
COL = (((1,), (0,)), ((), ()))
LIMIT = 56 * 1024 * 1024
COST = pl.CostEstimate(flops=36_000_000_000, transcendentals=0, bytes_accessed=8_000_000)
PAIR_COST = pl.CostEstimate(flops=14_000_000_000, transcendentals=0, bytes_accessed=4_000_000)


def dot(a, b, dims=COL):
    return lax.dot_general(a, b, dims, preferred_element_type=F32)


def normalize(inputs):
    center = inputs - jnp.mean(inputs, axis=-1, keepdims=True)
    factor = lax.rsqrt(jnp.mean(center * center, axis=-1, keepdims=True) + EPSILON)
    return (center * factor, factor)


def norm_back(upstream, normed, factor, gain):
    scaled = upstream * gain
    return factor * (
        scaled
        - jnp.mean(scaled, axis=-1, keepdims=True)
        - normed * jnp.mean(scaled * normed, axis=-1, keepdims=True)
    )


def segment_of(places, b1, b2):
    return (places >= b1).astype(jnp.int32) + (places >= b2).astype(jnp.int32)


def key_range(first, last, b1, b2, total):
    lo = jnp.where(first >= b2, b2, jnp.where(first >= b1, b1, 0))
    hi = jnp.where(last >= b2, total, jnp.where(last >= b1, b2, b1))
    return lo, hi


def half_mask(rows, side):
    lane = lax.broadcasted_iota(jnp.int32, (rows, 128), 1)
    return (lane < 64) if side == 0 else (lane >= 64)


def pick(pair, side):
    return jnp.where(half_mask(pair.shape[0], side), pair, jnp.zeros_like(pair))


def fill_bias(bias_ref, kb_ref, first, b1, b2, j0, j1):
    rows = first + lax.broadcasted_iota(jnp.int32, (BQ, 1), 0)
    row_seg = segment_of(rows, b1, b2)

    def body(j, carry):
        cols = j * BK + lax.broadcasted_iota(jnp.int32, (1, BK), 1)
        col_seg = segment_of(cols, b1, b2)
        kept = jnp.where(rows == cols, 0.0, jnp.broadcast_to(kb_ref[j], (BQ, BK)))
        bias_ref[j] = jnp.where(row_seg == col_seg, kept, NEG)
        return carry

    lax.fori_loop(j0, j1, body, 0)


def attend_kernel(s_ref, q_ref, k_ref, v_ref, kb_ref, o_ref, lse_ref, lset_ref, score, bias):
    total = k_ref.shape[0]
    pairs = q_ref.shape[1] // 128
    b1, b2 = s_ref[0], s_ref[1]
    first = s_ref[2] + pl.program_id(0) * BQ
    lo, hi = key_range(first, first + BQ - 1, b1, b2, total)
    j0, j1 = lo // BK, (hi + BK - 1) // BK
    fill_bias(bias, kb_ref, first, b1, b2, j0, j1)
    lane = lax.broadcasted_iota(jnp.int32, (BQ, 128), 1)
    lse_all = jnp.zeros((BQ, 128), F32)
    heads = 2 * pairs
    peak = None
    held = None
    for h in range(-1, heads):
        nxt = h + 1
        if nxt < heads:
            np_, ns = nxt // 2, nxt % 2
            q_head = pick(q_ref[:, np_ * 128 : np_ * 128 + 128], ns)
        if h >= 0:
            cp = h // 2

        def body(j, carry):
            top, tot, acc = carry
            rows = pl.ds(pl.multiple_of(j * BK, BK), BK)
            if nxt < heads:
                s = dot(q_head, k_ref[rows, np_ * 128 : np_ * 128 + 128], ROW) + bias[j]
                score[nxt % 2, j] = s
                top = jnp.maximum(top, jnp.maximum(s[:, :128], s[:, 128:]))
            if h >= 0:
                p = jnp.exp2(score[h % 2, j] - peak)
                tot = tot + (p[:, :128] + p[:, 128:])
                acc = acc + dot(p.astype(BF16), v_ref[rows, cp * 128 : cp * 128 + 128])
            return (top, tot, acc)

        start = (jnp.full((BQ, 128), NEG, F32), jnp.zeros((BQ, 128), F32), jnp.zeros((BQ, 128), F32))
        top, tot, acc = lax.fori_loop(j0, j1, body, start)
        if h >= 0:
            whole = jnp.sum(tot, axis=1, keepdims=True)
            result = acc / whole
            lse_all = jnp.where(lane == h, peak + jnp.log2(whole), lse_all)
            if h % 2 == 0:
                held = result
            else:
                o_ref[:, cp * 128 : cp * 128 + 128] = jnp.where(lane < 64, held, result).astype(BF16)
        peak = jnp.max(top, axis=1, keepdims=True)
    lse_ref[...] = lse_all
    lset_ref[...] = jnp.transpose(lse_all)[: lset_ref.shape[0], :]


def attend(scalars, qkv, kb, rows, pairs):
    total = qkv.shape[0]
    width = pairs * 128
    return pl.pallas_call(
        attend_kernel,
        grid_spec=pltpu.PrefetchScalarGridSpec(
            num_scalar_prefetch=1,
            grid=(rows // BQ,),
            in_specs=[
                pl.BlockSpec((BQ, width), lambda i, s: (s[2] // BQ + i, 0)),
                pl.BlockSpec((total, width), lambda i, s: (0, 1), pipeline_mode=pl.Buffered(1)),
                pl.BlockSpec((total, width), lambda i, s: (0, 2), pipeline_mode=pl.Buffered(1)),
                pl.BlockSpec((total // BK, 1, BK), lambda i, s: (0, 0, 0)),
            ],
            out_specs=[
                pl.BlockSpec((BQ, width), lambda i, s: (i, 0)),
                pl.BlockSpec((BQ, 128), lambda i, s: (i, 0)),
                pl.BlockSpec((8, BQ), lambda i, s: (0, i)),
            ],
            scratch_shapes=[
                pltpu.VMEM((2, total // BK, BQ, BK), F32),
                pltpu.VMEM((total // BK, BQ, BK), F32),
            ],
        ),
        out_shape=[
            jax.ShapeDtypeStruct((rows, width), BF16),
            jax.ShapeDtypeStruct((rows, 128), F32),
            jax.ShapeDtypeStruct((8, rows), F32),
        ],
        compiler_params=pltpu.CompilerParams(
            dimension_semantics=("arbitrary",), vmem_limit_bytes=LIMIT
        ),
        cost_estimate=COST,
        name="attend",
    )(scalars, qkv, qkv, qkv, kb)


def query_kernel(s_ref, q_ref, k_ref, v_ref, do_ref, o_ref, lse_ref, kb_ref, dq_ref, bias):
    total = k_ref.shape[0]
    pairs = q_ref.shape[1] // 128
    b1, b2 = s_ref[0], s_ref[1]
    first = s_ref[2] + pl.program_id(0) * BQ
    lo, hi = key_range(first, first + BQ - 1, b1, b2, total)
    j0, j1 = lo // BK, (hi + BK - 1) // BK
    fill_bias(bias, kb_ref, first, b1, b2, j0, j1)
    low = half_mask(BQ, 0)
    for p in range(pairs):
        span = slice(p * 128, p * 128 + 128)
        grads = do_ref[:, span]
        product = grads.astype(F32) * o_ref[:, span].astype(F32)
        sides = []
        for side in range(2):
            h = 2 * p + side
            sides.append(
                (
                    pick(q_ref[:, span], side),
                    pick(grads, side),
                    jnp.sum(pick(product, side), axis=1, keepdims=True),
                    lse_ref[:, h : h + 1],
                )
            )

        def body(j, accs):
            rows = pl.ds(pl.multiple_of(j * BK, BK), BK)
            keys = k_ref[rows, span]
            values = v_ref[rows, span]
            out = []
            for (qh, gh, delta, lse), acc in zip(sides, accs):
                prob = jnp.exp2(dot(qh, keys, ROW) + bias[j] - lse)
                score = (prob * (dot(gh, values, ROW) - delta)).astype(BF16)
                out.append(acc + dot(score, keys))
            return tuple(out)

        zero = jnp.zeros((BQ, 128), F32)
        left, right = lax.fori_loop(j0, j1, body, (zero, zero))
        dq_ref[:, span] = (jnp.where(low, left, right) * 0.125).astype(BF16)


def query_grads(scalars, qkv, dout, att, lse, kb, rows, pairs):
    total = qkv.shape[0]
    width = pairs * 128
    return pl.pallas_call(
        query_kernel,
        grid_spec=pltpu.PrefetchScalarGridSpec(
            num_scalar_prefetch=1,
            grid=(rows // BQ,),
            in_specs=[
                pl.BlockSpec((BQ, width), lambda i, s: (s[2] // BQ + i, 0)),
                pl.BlockSpec((total, width), lambda i, s: (0, 1), pipeline_mode=pl.Buffered(1)),
                pl.BlockSpec((total, width), lambda i, s: (0, 2), pipeline_mode=pl.Buffered(1)),
                pl.BlockSpec((BQ, width), lambda i, s: (i, 0)),
                pl.BlockSpec((BQ, width), lambda i, s: (i, 0)),
                pl.BlockSpec((BQ, 128), lambda i, s: (i, 0)),
                pl.BlockSpec((total // BK, 1, BK), lambda i, s: (0, 0, 0)),
            ],
            out_specs=pl.BlockSpec((BQ, width), lambda i, s: (i, 0)),
            scratch_shapes=[pltpu.VMEM((total // BK, BQ, BK), F32)],
        ),
        out_shape=jax.ShapeDtypeStruct((rows, width), BF16),
        compiler_params=pltpu.CompilerParams(
            dimension_semantics=("arbitrary",), vmem_limit_bytes=LIMIT
        ),
        cost_estimate=COST,
        name="query_grads",
    )(scalars, qkv, qkv, qkv, dout, att, lse, kb)


def key_kernel(s_ref, k_ref, v_ref, q_ref, do_ref, stat_ref, mask_ref, dk_ref, dv_ref, *, pair, per):
    total = q_ref.shape[0]
    b1, b2 = s_ref[0], s_ref[1]
    first = s_ref[2] + pl.program_id(0) * BK
    lo, hi = key_range(first, first + BK - 1, b1, b2, total)
    j0, j1 = lo // BQ, (hi + BQ - 1) // BQ
    rows = first + lax.broadcasted_iota(jnp.int32, (BK, 1), 0)
    row_seg = segment_of(rows, b1, b2)
    masked = jnp.transpose(jnp.broadcast_to(mask_ref[0], (128, BK)))[:, :1]
    sides = [(pick(k_ref[...], side), pick(v_ref[...], side)) for side in range(2)]

    def body(j, carry):
        span = pl.ds(pl.multiple_of(j * BQ, BQ), BQ)
        cols = j * BQ + lax.broadcasted_iota(jnp.int32, (1, BQ), 1)
        col_seg = segment_of(cols, b1, b2)
        bias = jnp.where(row_seg == col_seg, jnp.where(rows == cols, 0.0, masked), NEG)
        queries = q_ref[span, :]
        grads = do_ref[span, :]
        place = ((j // per) ^ s_ref[3]) * per + lax.rem(j, per)
        spot = pl.ds(pl.multiple_of(place * BQ, BQ), BQ)
        out = []
        for side in range(2):
            h = 2 * pair + side
            kh, vh = sides[side]
            dk, dv = carry[2 * side], carry[2 * side + 1]
            prob = jnp.exp2(dot(kh, queries, ROW) + bias - stat_ref[h : h + 1, spot])
            score = prob * (dot(vh, grads, ROW) - stat_ref[8 + h : 9 + h, spot])
            out.append(dk + dot(score.astype(BF16), queries))
            out.append(dv + dot(prob.astype(BF16), grads))
        return tuple(out)

    zero = jnp.zeros((BK, 128), F32)
    k0, v0, k1, v1 = lax.fori_loop(j0, j1, body, (zero, zero, zero, zero))
    low = half_mask(BK, 0)
    dk_ref[...] = (jnp.where(low, k0, k1) * (1.0 / LOG2E)).astype(BF16)
    dv_ref[...] = jnp.where(low, v0, v1).astype(BF16)


def key_grads(scalars, qkv, dout, stats, kb, rows, pairs, pair):
    total = qkv.shape[0]

    def kernel(*refs):
        key_kernel(*refs, pair=pair, per=rows // BQ)

    return pl.pallas_call(
        kernel,
        grid_spec=pltpu.PrefetchScalarGridSpec(
            num_scalar_prefetch=1,
            grid=(rows // BK,),
            in_specs=[
                pl.BlockSpec((BK, 128), lambda i, s: (s[2] // BK + i, pairs + pair)),
                pl.BlockSpec((BK, 128), lambda i, s: (s[2] // BK + i, 2 * pairs + pair)),
                pl.BlockSpec((total, 128), lambda i, s: (0, pair), pipeline_mode=pl.Buffered(1)),
                pl.BlockSpec((total, 128), lambda i, s: (0, pair), pipeline_mode=pl.Buffered(1)),
                pl.BlockSpec((16, total), lambda i, s: (0, 0), pipeline_mode=pl.Buffered(1)),
                pl.BlockSpec((1, 1, BK), lambda i, s: (s[2] // BK + i, 0, 0)),
            ],
            out_specs=[
                pl.BlockSpec((BK, 128), lambda i, s: (i, 0)),
                pl.BlockSpec((BK, 128), lambda i, s: (i, 0)),
            ],
        ),
        out_shape=[jax.ShapeDtypeStruct((rows, 128), BF16)] * 2,
        compiler_params=pltpu.CompilerParams(
            dimension_semantics=("arbitrary",), vmem_limit_bytes=LIMIT
        ),
        cost_estimate=PAIR_COST,
        name="key_grads",
    )(scalars, qkv, qkv, qkv, dout, stats, kb)


def put(out_ref, piece, height, start, low=0):
    unit = 192 if height % 192 == 0 else 16
    span = pl.ds(pl.multiple_of(start, unit), height)
    if len(piece.shape) == 3:
        wide = piece.shape[2]
        for k in range(piece.shape[0]):
            out_ref[span, k * wide : (k + 1) * wide] = piece[k]
    else:
        wide = out_ref.shape[1]
        out_ref[span, :] = piece[:height, low : low + wide]


def whole_spec(value):
    zeros = (0,) * value.ndim
    return pl.BlockSpec(value.shape, lambda i, s: zeros, pipeline_mode=pl.Buffered(1))


def place(scalars, pieces, spots, total, cuts):
    count = len(pieces)

    def kernel(s_ref, *refs):
        for i in range(count):
            height, start = spots[i](s_ref)
            for k, (low, wide) in enumerate(cuts):
                put(refs[count + k], refs[i], height, start, low)

    return pl.pallas_call(
        kernel,
        grid_spec=pltpu.PrefetchScalarGridSpec(
            num_scalar_prefetch=1,
            grid=(1,),
            in_specs=[whole_spec(piece) for piece in pieces],
            out_specs=[pl.BlockSpec((total, wide), lambda i, s: (0, 0)) for _, wide in cuts],
        ),
        out_shape=[jax.ShapeDtypeStruct((total, wide), BF16) for _, wide in cuts],
        compiler_params=pltpu.CompilerParams(vmem_limit_bytes=LIMIT),
        name="place",
    )(scalars, *pieces)


def project(scalars, pieces, spots, total, weights, wspots, bias=None, scale=None):
    count, wcount = len(pieces), len(weights)
    depth = pieces[0].shape[1]
    last = weights[0]
    cols = last.shape[1] if last.ndim == 2 else last.shape[0] * last.shape[2]
    block = 512
    extra = [] if bias is None else [bias, scale]
    keep = bias is not None

    def kernel(s_ref, *refs):
        ins, ws = refs[:count], refs[count : count + wcount]
        rest = refs[count + wcount :]
        if keep:
            bias_ref, scale_ref, out_ref, w_ref, x_ref = rest
        else:
            out_ref, x_ref = rest
            w_ref = ws[0]
        step = pl.program_id(0)

        @pl.when(step == 0)
        def _():
            for i in range(count):
                height, start = spots[i](s_ref)
                put(x_ref, ins[i], height, start)
            if keep:
                for i in range(wcount):
                    height, start = wspots[i](s_ref)
                    put(w_ref, ws[i], height, start)

        span = pl.ds(pl.multiple_of(step * block, block), block)
        value = dot(x_ref[span, :], w_ref[...])
        if keep:
            value = (value + bias_ref[...]) * scale_ref[...]
        out_ref[...] = value.astype(BF16)

    out_specs = [pl.BlockSpec((block, cols), lambda i, s: (i, 0))]
    out_shape = [jax.ShapeDtypeStruct((total, cols), BF16)]
    if keep:
        out_specs.append(pl.BlockSpec((depth, cols), lambda i, s: (0, 0)))
        out_shape.append(jax.ShapeDtypeStruct((depth, cols), BF16))
    return pl.pallas_call(
        kernel,
        grid_spec=pltpu.PrefetchScalarGridSpec(
            num_scalar_prefetch=1,
            grid=(total // block,),
            in_specs=[whole_spec(piece) for piece in pieces + weights + extra],
            out_specs=out_specs,
            scratch_shapes=[pltpu.VMEM((total, depth), BF16)],
        ),
        out_shape=out_shape,
        compiler_params=pltpu.CompilerParams(
            dimension_semantics=("arbitrary",), vmem_limit_bytes=LIMIT
        ),
        cost_estimate=pl.CostEstimate(
            flops=2 * total * depth * cols, transcendentals=0, bytes_accessed=4_000_000
        ),
        name="project",
    )(scalars, *pieces, *weights, *extra)


def split(value):
    high = lax.reduce_precision(value, 8, 7)
    return high.astype(BF16), (value - high).astype(BF16)


def after(value, *others):
    return lax.optimization_barrier((value, others))[0]


def solution(mesh):
    n_fsdp, n_context = mesh.shape["fsdp"], mesh.shape["context"]
    direct_f, direct_c = n_fsdp == 4, n_context == 4
    swap = [(0, 1), (1, 0)]

    def partner(value, axis, d):
        return lax.ppermute(value, axis, [(i, i ^ d) for i in range(4)])

    def twin(value):
        return lax.ppermute(value, "tensor", swap)

    def pair_sum(value):
        low = value.astype(BF16)
        return low.astype(F32) + twin(low).astype(F32)

    def send_weight(shard, axis=0):
        if not direct_f:
            return [lax.all_gather(shard, "fsdp", axis=axis, tiled=True)]
        return [shard] + [partner(shard, "fsdp", d) for d in (1, 2, 3)]

    def weight_spots(pieces, axis=0):
        rows = pieces[0].shape[axis]
        if not direct_f:
            return [lambda s: (rows, 0)]
        return [lambda s, d=d: (rows, (s[6] ^ d) * rows) for d in range(4)]

    def send_rows(block, stats=None):
        if not direct_c:
            whole = lax.all_gather(block, "context", axis=0, tiled=True)
            if stats is None:
                return [whole]
            return [whole, lax.all_gather(stats, "context", axis=1, tiled=True)]
        half = block.shape[0] // 2
        mine = lax.dynamic_slice_in_dim(block, lax.axis_index("tensor") * half, half, 0)
        if stats is not None:
            mine = jnp.concatenate((mine,) + split(stats), axis=0)
        near = partner(mine, "context", 1)
        far = partner(mine, "context", 2)
        inner = lax.ppermute(mine, "context", [(1, 2), (2, 1)])
        return [near, far, inner]

    def row_pieces(block, got):
        if not direct_c:
            rows = got[0].shape[0]
            return got[:1], [lambda s: (rows, 0)]
        rows = block.shape[0]
        half = rows // 2
        pieces, spots = [block], [lambda s: (rows, s[4] * rows)]
        for d in (1, 2, 3):
            pieces.append(got[d - 1])
            spots.append(lambda s, d=d: (half, (s[4] ^ d) * rows + s[5] * half))
            pieces.append(twin(got[d - 1]))
            spots.append(lambda s, d=d: (half, (s[4] ^ d) * rows + (1 - s[5]) * half))
        return pieces, spots

    def row_stats(stats, got, half):
        if not direct_c:
            return got[1]
        both = [piece[half : half + 16].astype(F32) + piece[half + 16 :].astype(F32) for piece in got]
        return jnp.concatenate([stats] + both, axis=1)

    def pack(small, cols):
        high, low = split(small)
        filler = jnp.zeros((16 - 2 * small.shape[0], cols), BF16)
        return jnp.concatenate([high, low, filler], axis=0)

    def unpack(block, rows):
        return block[:rows].astype(F32) + block[rows : 2 * rows].astype(F32)

    def send_f(partials, small=None):
        if not direct_f:
            whole = jnp.concatenate(partials, axis=1)
            share = lax.psum_scatter(whole, "fsdp", scatter_dimension=0, tiled=True)
            return [share], None if small is None else lax.psum(small, "fsdp")
        me, rows = lax.axis_index("fsdp"), partials[0].shape[0] // 4
        cols = sum([partial.shape[1] for partial in partials])
        extra = [] if small is None else [pack(small, cols)]
        blocks = []
        for d in range(4):
            cut = [lax.dynamic_slice_in_dim(p, (me ^ d) * rows, rows, 0) for p in partials]
            piece = jnp.concatenate(cut, axis=1) if len(cut) > 1 else cut[0]
            if d:
                piece = jnp.concatenate([piece] + extra, axis=0) if extra else piece
                piece = partner(piece, "fsdp", d)
            blocks.append(piece)
        return blocks, small

    def finish_f(blocks, small=None):
        if not direct_f:
            return blocks[0], small
        rows = blocks[0].shape[0]
        parts = [block[:rows].astype(F32) for block in blocks]
        share = ((parts[0] + parts[1]) + (parts[2] + parts[3])).astype(BF16)
        if small is None:
            return share, None
        more = [unpack(block[rows:], small.shape[0]) for block in blocks[1:]]
        return share, (small + more[0]) + (more[1] + more[2])

    def send_z(mine, theirs, small, d):
        if small is not None:
            theirs = jnp.concatenate([theirs, pack(small, mine.shape[1])], axis=0)
        return (mine, partner(theirs, "context", d), small)

    def send_1(share, small=None):
        if not direct_c:
            return (share, small)
        side, rows = lax.rem(lax.axis_index("context"), 2), share.shape[0] // 2
        mine = lax.dynamic_slice_in_dim(share, side * rows, rows, 0)
        theirs = lax.dynamic_slice_in_dim(share, (1 - side) * rows, rows, 0)
        return send_z(mine, theirs, small, 1)

    def finish_z(state):
        if not direct_c:
            return state
        mine, got, small = state
        rows = mine.shape[0]
        total = (mine.astype(F32) + got[:rows].astype(F32)).astype(BF16)
        if small is not None:
            small = small + unpack(got[rows:], small.shape[0])
        return total, small

    def send_2(share, small=None):
        if not direct_c:
            return (share, small)
        return send_z(share, share, small, 2)

    def send_3(share, small=None):
        if not direct_c:
            total = lax.psum(share, "context")
            return (total, None if small is None else lax.psum(small, "context"))
        return (share, partner(share, "context", 1), small)

    def finish_3(state):
        if not direct_c:
            return state[0].astype(F32), state[1]
        share, other, small = state
        side = lax.rem(lax.axis_index("context"), 2)
        first = jnp.where(side == 0, share, other)
        second = jnp.where(side == 0, other, share)
        return jnp.concatenate([first, second], axis=0).astype(F32), small

    def shards(
        tokens,
        cotangent,
        w_qkv,
        bias_qv,
        w_attn_out,
        w_up,
        bias_up,
        w_down,
        gains,
        shifts,
        seq_lengths,
        key_mask,
    ):
        rows = tokens.shape[0]
        width = w_qkv.shape[2]
        pairs = width // 128
        hidden = w_up.shape[1]
        total = key_mask.shape[0]
        dim = tokens.shape[1]
        b1 = seq_lengths[0, 0]
        b2 = b1 + seq_lengths[0, 1]
        me = lax.axis_index("context")
        order = me if direct_c else 0 * me
        scalars = jnp.stack(
            [b1, b2, me * rows, order, me, lax.axis_index("tensor"), lax.axis_index("fsdp")]
        ).astype(jnp.int32)
        kb = jnp.where(key_mask == 1, 0.0, NEG).astype(F32).reshape(total // BK, 1, BK)

        got = send_rows(tokens)
        wq = send_weight(w_qkv, 1)
        got, wq = lax.optimization_barrier((got, wq))
        shard = jnp.concatenate([w_attn_out.T, w_up, w_down.T], axis=1)
        rest = send_weight(after(shard, wq[-1]))
        cuts = [(0, width), (width, hidden), (width + hidden, hidden)]
        zero = jnp.zeros((width,), F32)
        bias_row = jnp.concatenate([bias_qv[0], zero, bias_qv[1]]).reshape(1, -1)
        scale_row = jnp.concatenate([zero + 0.125 * LOG2E, zero + 1.0, zero + 1.0]).reshape(1, -1)
        pieces, spots = row_pieces(tokens, got)
        qkv, w_proj = project(
            scalars, pieces, spots, total, wq, weight_spots(wq, 1), bias_row, scale_row
        )
        attended, lse, lset = attend(scalars, qkv, kb, rows, pairs)
        rest = after(rest, attended)
        w_back, w_upper, w_lower = place(scalars, rest, weight_spots(rest), dim, cuts)

        branch = pair_sum(dot(attended, w_back, ROW))
        first_sum = tokens.astype(F32) + branch + shifts[0]
        normed1, factor1 = normalize(first_sum)
        first = normed1 * gains[0] + shifts[1]
        first_low = first.astype(BF16)
        upper = dot(first_low, w_upper) + bias_up
        active_f, gelu_back = jax.vjp(lambda values: jax.nn.gelu(values, approximate=False), upper)
        active = active_f.astype(BF16)
        second_sum = first + pair_sum(dot(active, w_lower, ROW)) + shifts[2]
        normed2, factor2 = normalize(second_sum)
        out = (normed2 * gains[1] + shifts[3]).astype(BF16)
        upstream = cotangent.astype(F32)
        gain_two = jnp.sum(upstream * normed2, axis=0)
        shift_three = jnp.sum(upstream, axis=0)
        grad_second = norm_back(upstream, normed2, factor2, gains[1])
        shift_two = jnp.sum(grad_second, axis=0)
        lower_grad = grad_second.astype(BF16)
        group_a, _ = send_f([dot(lower_grad.T, active).astype(BF16)])
        grad_active = dot(lower_grad, w_lower)
        grad_upper = gelu_back(grad_active)[0].astype(BF16)
        grad_bias_up = jnp.sum(grad_upper.astype(F32), axis=0)
        grad_first = grad_second + pair_sum(dot(grad_upper, w_upper, ROW))
        gain_one = jnp.sum(grad_first * normed1, axis=0)
        shift_one = jnp.sum(grad_first, axis=0)
        grad_first_sum = norm_back(grad_first, normed1, factor1, gains[0])
        shift_zero = jnp.sum(grad_first_sum, axis=0)
        branch_grad = grad_first_sum.astype(BF16)

        dout = dot(branch_grad, w_back).astype(BF16)
        marks = np.zeros((8, width), np.float32)
        for h in range(width // 64):
            marks[h, h * 64 : h * 64 + 64] = 1.0
        product = dout.astype(F32) * attended.astype(F32)
        deltat = lax.dot_general(
            jnp.asarray(marks), product, ROW, precision=lax.Precision.HIGHEST,
            preferred_element_type=F32,
        )
        stats = jnp.concatenate([lset, deltat], axis=0)
        got = send_rows(branch_grad, stats)
        small = jnp.concatenate(
            [gain_one, gain_two, shift_zero, shift_one, shift_two, shift_three, grad_bias_up]
        ).reshape(-1, hidden)
        group_b, small = send_f([dot(first_low.T, grad_upper).astype(BF16)], small)
        dq = query_grads(scalars, qkv, dout, attended, lse, kb, rows, pairs)

        got = after(got, dq)
        stats_all = row_stats(stats, got, rows // 2)
        pieces, spots = row_pieces(branch_grad, got)
        (dout_all,) = project(scalars, pieces, spots, total, [w_back], None)
        group_a, _ = finish_f(after(group_a, dq))
        group_b, small = finish_f(after(group_b, dq), small)
        state_a, state_b = send_1(group_a), send_1(group_b, small)
        dks, dvs = [], []
        gate = (group_a, group_b)
        for pair in range(pairs):
            dk, dv = key_grads(
                after(scalars, gate), qkv, dout_all, stats_all, kb, rows, pairs, pair
            )
            dks.append(dk)
            dvs.append(dv)
            if pair == 0:
                group_a, group_b = finish_z(after(state_a, dk)), finish_z(after(state_b, dk))
                state_a, state_b = send_2(*group_a), send_2(*group_b)
                gate = (group_a, group_b)
            elif pair == 1:
                group_a, group_b = finish_z(after(state_a, dk)), finish_z(after(state_b, dk))
                state_a, state_b = send_3(*group_a), send_3(*group_b)
                early = jnp.concatenate([dq] + dks + dvs, axis=1)
                sums = jnp.sum(early.astype(F32), axis=0, keepdims=True)
                row = jnp.pad(sums, ((0, 0), (0, width)))
                group_c, row = send_f(
                    [
                        dot(tokens.T, early).astype(BF16),
                        dot(branch_grad.T, attended).astype(BF16),
                    ],
                    row,
                )
                gate = (group_a, group_b)
        late = jnp.concatenate([dks[-1], dvs[-1]], axis=1)
        tail = jnp.sum(late.astype(F32), axis=0, keepdims=True)
        group_d, tail = send_f([dot(tokens.T, late).astype(BF16)], tail)
        group_c, row = finish_f(after(group_c, late), row)
        state_c = send_1(group_c, row)
        stacked = jnp.concatenate([dq] + dks + dvs, axis=1)
        input_part = pair_sum(dot(stacked, w_proj, ROW))
        grad_tokens = (grad_first_sum + input_part).astype(BF16)
        group_d, tail = finish_f(group_d, tail)
        state_d = send_1(group_d, tail)
        state_c, state_d = send_2(*finish_z(state_c)), send_2(*finish_z(state_d))
        group_a, _ = finish_3(after(state_a, late))
        group_b, small = finish_3(after(state_b, late))
        state_c, state_d = send_3(*finish_z(state_c)), send_3(*finish_z(state_d))
        group_c, row = finish_3(state_c)
        group_d, tail = finish_3(state_d)

        small = small.reshape(-1)
        sum_gains = small[: 2 * dim].reshape(2, dim)
        sum_shifts = small[2 * dim : 6 * dim].reshape(4, dim)
        sum_bias_up = small[6 * dim :]
        near_k = width + width - 128
        near_v = near_k + width - 128
        sum_bias_qv = jnp.stack(
            [row[0, :width], jnp.concatenate([row[0, near_k:near_v], tail[0, 128:]])]
        )
        share_qkv = jnp.stack(
            [
                group_c[:, :width],
                jnp.concatenate([group_c[:, width:near_k], group_d[:, :128]], axis=1),
                jnp.concatenate([group_c[:, near_k:near_v], group_d[:, 128:]], axis=1),
            ]
        )
        share_lower = group_a.T
        share_upper = group_b
        share_back = group_c[:, near_v:].T
        return (
            out,
            grad_tokens,
            share_qkv,
            share_back,
            share_upper,
            share_lower,
            sum_bias_qv,
            sum_bias_up,
            sum_gains,
            sum_shifts,
        )

    return jax.shard_map(
        shards,
        mesh=mesh,
        in_specs=(
            P(("fsdp", "context"), None),
            P(("fsdp", "context"), None),
            P(None, "fsdp", "tensor"),
            P(None, "tensor"),
            P("tensor", "fsdp"),
            P("fsdp", "tensor"),
            P("tensor"),
            P("tensor", "fsdp"),
            P(),
            P(),
            P("fsdp", None),
            P("fsdp"),
        ),
        out_specs=(
            P(("fsdp", "context"), None),
            P(("fsdp", "context"), None),
            P(None, "fsdp", "tensor"),
            P("tensor", "fsdp"),
            P("fsdp", "tensor"),
            P("tensor", "fsdp"),
            P(None, "tensor"),
            P("tensor"),
            P(),
            P(),
        ),
        check_vma=False,
    )
```

```python
import jax
import jax.numpy as jnp
import numpy as np
from jax import lax
from jax.experimental import pallas as pl
from jax.experimental.pallas import tpu as pltpu
from jax.sharding import PartitionSpec as P

EPSILON = 1e-12
LOG2E = 1.4426950408889634
NEG = -1e30
BQ = 256
BK = 256
F32 = jnp.float32
BF16 = jnp.bfloat16
ROW = (((1,), (1,)), ((), ()))
COL = (((1,), (0,)), ((), ()))
LIMIT = 56 * 1024 * 1024
COST = pl.CostEstimate(flops=36_000_000_000, transcendentals=0, bytes_accessed=8_000_000)
PAIR_COST = pl.CostEstimate(flops=14_000_000_000, transcendentals=0, bytes_accessed=4_000_000)


def dot(a, b, dims=COL):
    return lax.dot_general(a, b, dims, preferred_element_type=F32)


def normalize(inputs):
    center = inputs - jnp.mean(inputs, axis=-1, keepdims=True)
    factor = lax.rsqrt(jnp.mean(center * center, axis=-1, keepdims=True) + EPSILON)
    return (center * factor, factor)


def norm_back(upstream, normed, factor, gain):
    scaled = upstream * gain
    return factor * (
        scaled
        - jnp.mean(scaled, axis=-1, keepdims=True)
        - normed * jnp.mean(scaled * normed, axis=-1, keepdims=True)
    )


def segment_of(places, b1, b2):
    return (places >= b1).astype(jnp.int32) + (places >= b2).astype(jnp.int32)


def key_range(first, last, b1, b2, total):
    lo = jnp.where(first >= b2, b2, jnp.where(first >= b1, b1, 0))
    hi = jnp.where(last >= b2, total, jnp.where(last >= b1, b2, b1))
    return lo, hi


def half_mask(rows, side):
    lane = lax.broadcasted_iota(jnp.int32, (rows, 128), 1)
    return (lane < 64) if side == 0 else (lane >= 64)


def pick(pair, side):
    return jnp.where(half_mask(pair.shape[0], side), pair, jnp.zeros_like(pair))


def column(row):
    return jnp.transpose(jnp.broadcast_to(row, (128, row.shape[1])))[:, :1]


def fill_bias(bias_ref, kb_ref, first, b1, b2, j0, j1):
    cols = first + lax.broadcasted_iota(jnp.int32, (1, BQ), 1)
    col_seg = segment_of(cols, b1, b2)

    def body(j, carry):
        rows = j * BK + lax.broadcasted_iota(jnp.int32, (BK, 1), 0)
        row_seg = segment_of(rows, b1, b2)
        kept = jnp.where(rows == cols, 0.0, jnp.broadcast_to(column(kb_ref[j]), (BK, BQ)))
        bias_ref[j] = jnp.where(row_seg == col_seg, kept, NEG)
        return carry

    lax.fori_loop(j0, j1, body, 0)


def attend_kernel(s_ref, q_ref, k_ref, v_ref, kb_ref, o_ref, lset_ref, score, bias):
    total = k_ref.shape[0]
    pairs = q_ref.shape[1] // 128
    b1, b2 = s_ref[0], s_ref[1]
    first = s_ref[2] + pl.program_id(0) * BQ
    lo, hi = key_range(first, first + BQ - 1, b1, b2, total)
    j0, j1 = lo // BK, (hi + BK - 1) // BK
    fill_bias(bias, kb_ref, first, b1, b2, j0, j1)
    peaks = None
    for p in range(-1, pairs):
        nxt = p + 1
        if nxt < pairs:
            ahead = slice(nxt * 128, nxt * 128 + 128)
            heads = [pick(q_ref[:, ahead], side) for side in range(2)]
        here = slice(p * 128, p * 128 + 128)

        def body(j, carry):
            tops, tots, accs = [list(part) for part in carry]
            rows = pl.ds(pl.multiple_of(j * BK, BK), BK)
            if nxt < pairs:
                keys = k_ref[rows, ahead]
                for side in range(2):
                    s = dot(keys, heads[side], ROW) + bias[j]
                    score[nxt % 2, side, j] = s
                    tops[side] = jnp.maximum(tops[side], jnp.max(s.reshape(BK // 8, 8, BQ), axis=0))
            if p >= 0:
                turned = jnp.transpose(v_ref[rows, here])
                for side in range(2):
                    prob = jnp.exp2(score[p % 2, side, j] - peaks[side])
                    tots[side] = tots[side] + jnp.sum(prob.reshape(BK // 8, 8, BQ), axis=0)
                    accs[side] = accs[side] + dot(
                        turned[64 * side : 64 * side + 64], prob.astype(BF16)
                    )
            return (tuple(tops), tuple(tots), tuple(accs))

        low, zero, wide = jnp.full((8, BQ), NEG, F32), jnp.zeros((8, BQ), F32), jnp.zeros((64, BQ), F32)
        tops, tots, accs = lax.fori_loop(j0, j1, body, ((low, low), (zero, zero), (wide, wide)))
        if p >= 0:
            results = []
            for side in range(2):
                h = 2 * p + side
                whole = jnp.sum(tots[side], axis=0, keepdims=True)
                results.append(accs[side] * (1.0 / whole))
                lset_ref[h : h + 1, :] = peaks[side] + jnp.log2(whole)
            o_ref[:, here] = jnp.transpose(jnp.concatenate(results, axis=0)).astype(BF16)
        peaks = [jnp.max(top, axis=0, keepdims=True) for top in tops]


def attend(scalars, qkv, kb, rows, pairs):
    total = qkv.shape[0]
    width = pairs * 128
    return pl.pallas_call(
        attend_kernel,
        grid_spec=pltpu.PrefetchScalarGridSpec(
            num_scalar_prefetch=1,
            grid=(rows // BQ,),
            in_specs=[
                pl.BlockSpec((BQ, width), lambda i, s: (s[2] // BQ + i, 0)),
                pl.BlockSpec((total, width), lambda i, s: (0, 1), pipeline_mode=pl.Buffered(1)),
                pl.BlockSpec((total, width), lambda i, s: (0, 2), pipeline_mode=pl.Buffered(1)),
                pl.BlockSpec((total // BK, 1, BK), lambda i, s: (0, 0, 0)),
            ],
            out_specs=[
                pl.BlockSpec((BQ, width), lambda i, s: (i, 0)),
                pl.BlockSpec((8, BQ), lambda i, s: (0, i)),
            ],
            scratch_shapes=[
                pltpu.VMEM((2, 2, total // BK, BK, BQ), F32),
                pltpu.VMEM((total // BK, BK, BQ), F32),
            ],
        ),
        out_shape=[
            jax.ShapeDtypeStruct((rows, width), BF16),
            jax.ShapeDtypeStruct((8, rows), F32),
        ],
        compiler_params=pltpu.CompilerParams(
            dimension_semantics=("arbitrary",), vmem_limit_bytes=LIMIT
        ),
        cost_estimate=COST,
        name="attend",
    )(scalars, qkv, qkv, qkv, kb)


def query_kernel(s_ref, q_ref, k_ref, v_ref, do_ref, stat_ref, kb_ref, dq_ref, bias):
    total = k_ref.shape[0]
    pairs = q_ref.shape[1] // 128
    b1, b2 = s_ref[0], s_ref[1]
    first = s_ref[2] + pl.program_id(0) * BQ
    lo, hi = key_range(first, first + BQ - 1, b1, b2, total)
    j0, j1 = lo // BK, (hi + BK - 1) // BK
    fill_bias(bias, kb_ref, first, b1, b2, j0, j1)
    for p in range(pairs):
        span = slice(p * 128, p * 128 + 128)
        sides = []
        for side in range(2):
            h = 2 * p + side
            sides.append(
                (
                    pick(q_ref[:, span], side),
                    pick(do_ref[:, span], side),
                    stat_ref[8 + h : 9 + h, :],
                    stat_ref[h : h + 1, :],
                )
            )

        def body(j, accs):
            rows = pl.ds(pl.multiple_of(j * BK, BK), BK)
            keys = k_ref[rows, span]
            values = v_ref[rows, span]
            turned = jnp.transpose(keys)
            out = []
            for side in range(2):
                qh, gh, delta, lse = sides[side]
                prob = jnp.exp2(dot(keys, qh, ROW) + bias[j] - lse)
                score = (prob * (dot(values, gh, ROW) - delta)).astype(BF16)
                out.append(accs[side] + dot(turned[64 * side : 64 * side + 64], score))
            return tuple(out)

        zero = jnp.zeros((64, BQ), F32)
        both = lax.fori_loop(j0, j1, body, (zero, zero))
        dq_ref[:, span] = (jnp.transpose(jnp.concatenate(both, axis=0)) * 0.125).astype(BF16)


def query_grads(scalars, qkv, dout, stats, kb, rows, pairs):
    total = qkv.shape[0]
    width = pairs * 128
    return pl.pallas_call(
        query_kernel,
        grid_spec=pltpu.PrefetchScalarGridSpec(
            num_scalar_prefetch=1,
            grid=(rows // BQ,),
            in_specs=[
                pl.BlockSpec((BQ, width), lambda i, s: (s[2] // BQ + i, 0)),
                pl.BlockSpec((total, width), lambda i, s: (0, 1), pipeline_mode=pl.Buffered(1)),
                pl.BlockSpec((total, width), lambda i, s: (0, 2), pipeline_mode=pl.Buffered(1)),
                pl.BlockSpec((BQ, width), lambda i, s: (i, 0)),
                pl.BlockSpec((16, BQ), lambda i, s: (0, i)),
                pl.BlockSpec((total // BK, 1, BK), lambda i, s: (0, 0, 0)),
            ],
            out_specs=pl.BlockSpec((BQ, width), lambda i, s: (i, 0)),
            scratch_shapes=[pltpu.VMEM((total // BK, BK, BQ), F32)],
        ),
        out_shape=jax.ShapeDtypeStruct((rows, width), BF16),
        compiler_params=pltpu.CompilerParams(
            dimension_semantics=("arbitrary",), vmem_limit_bytes=LIMIT
        ),
        cost_estimate=COST,
        name="query_grads",
    )(scalars, qkv, qkv, qkv, dout, stats, kb)


def key_kernel(s_ref, k_ref, v_ref, q_ref, do_ref, stat_ref, mask_ref, dk_ref, dv_ref, *, pair, per):
    total = q_ref.shape[0]
    b1, b2 = s_ref[0], s_ref[1]
    first = s_ref[2] + pl.program_id(0) * BK
    lo, hi = key_range(first, first + BK - 1, b1, b2, total)
    j0, j1 = lo // BQ, (hi + BQ - 1) // BQ
    rows = first + lax.broadcasted_iota(jnp.int32, (BK, 1), 0)
    row_seg = segment_of(rows, b1, b2)
    masked = column(mask_ref[0])

    def body(j, carry):
        dk, dv = carry
        span = pl.ds(pl.multiple_of(j * BQ, BQ), BQ)
        cols = j * BQ + lax.broadcasted_iota(jnp.int32, (1, BQ), 1)
        col_seg = segment_of(cols, b1, b2)
        bias = jnp.where(row_seg == col_seg, jnp.where(rows == cols, 0.0, masked), NEG)
        queries, grads = q_ref[span, :], do_ref[span, :]
        place = ((j // per) ^ s_ref[3]) * per + lax.rem(j, per)
        spot = pl.ds(pl.multiple_of(place * BQ, BQ), BQ)
        for side in range(2):
            h = 2 * pair + side
            qh, gh = pick(queries, side), pick(grads, side)
            prob = jnp.exp2(dot(k_ref[...], qh, ROW) + bias - stat_ref[h : h + 1, spot])
            score = prob * (dot(v_ref[...], gh, ROW) - stat_ref[8 + h : 9 + h, spot])
            dk = dk + dot(score.astype(BF16), qh)
            dv = dv + dot(prob.astype(BF16), gh)
        return dk, dv

    zero = jnp.zeros((BK, 128), F32)
    dk, dv = lax.fori_loop(j0, j1, body, (zero, zero))
    dk_ref[...] = (dk * (1.0 / LOG2E)).astype(BF16)
    dv_ref[...] = dv.astype(BF16)


def key_grads(scalars, qkv, dout, stats, kb, rows, pairs, pair):
    total = qkv.shape[0]

    def kernel(*refs):
        key_kernel(*refs, pair=pair, per=rows // BQ)

    return pl.pallas_call(
        kernel,
        grid_spec=pltpu.PrefetchScalarGridSpec(
            num_scalar_prefetch=1,
            grid=(rows // BK,),
            in_specs=[
                pl.BlockSpec((BK, 128), lambda i, s: (s[2] // BK + i, pairs + pair)),
                pl.BlockSpec((BK, 128), lambda i, s: (s[2] // BK + i, 2 * pairs + pair)),
                pl.BlockSpec((total, 128), lambda i, s: (0, pair), pipeline_mode=pl.Buffered(1)),
                pl.BlockSpec((total, 128), lambda i, s: (0, pair), pipeline_mode=pl.Buffered(1)),
                pl.BlockSpec((16, total), lambda i, s: (0, 0), pipeline_mode=pl.Buffered(1)),
                pl.BlockSpec((1, 1, BK), lambda i, s: (s[2] // BK + i, 0, 0)),
            ],
            out_specs=[
                pl.BlockSpec((BK, 128), lambda i, s: (i, 0)),
                pl.BlockSpec((BK, 128), lambda i, s: (i, 0)),
            ],
        ),
        out_shape=[jax.ShapeDtypeStruct((rows, 128), BF16)] * 2,
        compiler_params=pltpu.CompilerParams(
            dimension_semantics=("arbitrary",), vmem_limit_bytes=LIMIT
        ),
        cost_estimate=PAIR_COST,
        name="key_grads",
    )(scalars, qkv, qkv, qkv, dout, stats, kb)


def put(out_ref, piece, height, start, low=0):
    unit = 192 if height % 192 == 0 else 16
    span = pl.ds(pl.multiple_of(start, unit), height)
    if len(piece.shape) == 3:
        wide = piece.shape[2]
        for k in range(piece.shape[0]):
            out_ref[span, k * wide : (k + 1) * wide] = piece[k]
    else:
        wide = out_ref.shape[1]
        out_ref[span, :] = piece[:height, low : low + wide]


def whole_spec(value):
    zeros = (0,) * value.ndim
    return pl.BlockSpec(value.shape, lambda i, s: zeros, pipeline_mode=pl.Buffered(1))


def place(scalars, pieces, spots, total, cuts):
    count = len(pieces)

    def kernel(s_ref, *refs):
        for i in range(count):
            height, start = spots[i](s_ref)
            for k, (low, wide) in enumerate(cuts):
                put(refs[count + k], refs[i], height, start, low)

    return pl.pallas_call(
        kernel,
        grid_spec=pltpu.PrefetchScalarGridSpec(
            num_scalar_prefetch=1,
            grid=(1,),
            in_specs=[whole_spec(piece) for piece in pieces],
            out_specs=[pl.BlockSpec((total, wide), lambda i, s: (0, 0)) for _, wide in cuts],
        ),
        out_shape=[jax.ShapeDtypeStruct((total, wide), BF16) for _, wide in cuts],
        compiler_params=pltpu.CompilerParams(vmem_limit_bytes=LIMIT),
        name="place",
    )(scalars, *pieces)


def project(scalars, pieces, spots, total, weights, wspots, bias=None, scale=None):
    count, wcount = len(pieces), len(weights)
    depth = pieces[0].shape[1]
    last = weights[0]
    cols = last.shape[1] if last.ndim == 2 else last.shape[0] * last.shape[2]
    block = 512
    extra = [] if bias is None else [bias, scale]
    keep = bias is not None

    def kernel(s_ref, *refs):
        ins, ws = refs[:count], refs[count : count + wcount]
        rest = refs[count + wcount :]
        if keep:
            bias_ref, scale_ref, out_ref, w_ref, x_ref = rest
        else:
            out_ref, x_ref = rest
            w_ref = ws[0]
        step = pl.program_id(0)

        @pl.when(step == 0)
        def _():
            for i in range(count):
                height, start = spots[i](s_ref)
                put(x_ref, ins[i], height, start)
            if keep:
                for i in range(wcount):
                    height, start = wspots[i](s_ref)
                    put(w_ref, ws[i], height, start)

        span = pl.ds(pl.multiple_of(step * block, block), block)
        value = dot(x_ref[span, :], w_ref[...])
        if keep:
            value = (value + bias_ref[...]) * scale_ref[...]
        out_ref[...] = value.astype(BF16)

    out_specs = [pl.BlockSpec((block, cols), lambda i, s: (i, 0))]
    out_shape = [jax.ShapeDtypeStruct((total, cols), BF16)]
    if keep:
        out_specs.append(pl.BlockSpec((depth, cols), lambda i, s: (0, 0)))
        out_shape.append(jax.ShapeDtypeStruct((depth, cols), BF16))
    return pl.pallas_call(
        kernel,
        grid_spec=pltpu.PrefetchScalarGridSpec(
            num_scalar_prefetch=1,
            grid=(total // block,),
            in_specs=[whole_spec(piece) for piece in pieces + weights + extra],
            out_specs=out_specs,
            scratch_shapes=[pltpu.VMEM((total, depth), BF16)],
        ),
        out_shape=out_shape,
        compiler_params=pltpu.CompilerParams(
            dimension_semantics=("arbitrary",), vmem_limit_bytes=LIMIT
        ),
        cost_estimate=pl.CostEstimate(
            flops=2 * total * depth * cols, transcendentals=0, bytes_accessed=4_000_000
        ),
        name="project",
    )(scalars, *pieces, *weights, *extra)


def call_rows(kernel, rows, name, blocked, fixed, outs, kept=(), flops=0):
    specs = [pl.BlockSpec((BQ,) + v.shape[1:], lambda i: (i, 0)) for v in blocked]
    specs += [pl.BlockSpec(v.shape, lambda i: (0, 0), pipeline_mode=pl.Buffered(1)) for v in fixed]
    shapes, out_specs = [], []
    for wide, kind in outs:
        if kind == "turned":
            shapes.append(jax.ShapeDtypeStruct((8, rows), F32))
            out_specs.append(pl.BlockSpec((8, BQ), lambda i: (0, i)))
        else:
            shapes.append(jax.ShapeDtypeStruct((rows, wide), kind))
            out_specs.append(pl.BlockSpec((BQ, wide), lambda i: (i, 0)))
    for wide in kept:
        shapes.append(jax.ShapeDtypeStruct((8, wide), F32))
        out_specs.append(pl.BlockSpec((8, wide), lambda i: (0, 0)))
    return pl.pallas_call(
        kernel,
        grid=(rows // BQ,),
        in_specs=specs,
        out_specs=out_specs,
        out_shape=shapes,
        compiler_params=pltpu.CompilerParams(
            dimension_semantics=("arbitrary",), vmem_limit_bytes=LIMIT
        ),
        cost_estimate=pl.CostEstimate(flops=flops, transcendentals=0, bytes_accessed=4_000_000),
        name=name,
    )(*blocked, *fixed)


def upper_kernel(
    tok, mine, other, gains, shifts, bias, w_up, w_low, normed_ref, factor_ref, low_ref, active_ref, slope_ref, part_ref
):
    total = tok[...].astype(F32) + (mine[...].astype(F32) + other[...].astype(F32)) + shifts[0:1, :]
    normed, factor = normalize(total)
    normed_ref[...] = normed
    factor_ref[...] = jnp.broadcast_to(factor, factor_ref.shape)
    low = (normed * gains[0:1, :] + shifts[1:2, :]).astype(BF16)
    low_ref[...] = low
    acc = jnp.zeros(part_ref.shape, F32)
    step = 512
    for k in range(w_up.shape[1] // step):
        span = slice(k * step, k * step + step)
        upper = dot(low, w_up[:, span]) + bias[:, span]
        half = 0.5 + 0.5 * lax.erf(upper * 0.7071067811865476)
        bell = jnp.exp2(upper * upper * (-0.5 * LOG2E)) * 0.3989422804014327
        slope_ref[:, span] = half + upper * bell
        active = (upper * half).astype(BF16)
        active_ref[:, span] = active
        acc = acc + dot(active, w_low[:, span], ROW)
    part_ref[...] = acc.astype(BF16)


def lower_kernel(
    normed_ref, mine, other, cot, slope, gains, shifts, w_up, w_low, out_ref, grad_ref, low_ref, up_ref, part_ref, sum_ref
):
    first = normed_ref[...] * gains[0:1, :] + shifts[1:2, :]
    total = first + (mine[...].astype(F32) + other[...].astype(F32)) + shifts[2:3, :]
    normed, factor = normalize(total)
    out_ref[...] = (normed * gains[1:2, :] + shifts[3:4, :]).astype(BF16)
    upstream = cot[...].astype(F32)
    grad = norm_back(upstream, normed, factor, gains[1:2, :])
    grad_ref[...] = grad
    low = grad.astype(BF16)
    low_ref[...] = low
    dim = low.shape[1]

    @pl.when(pl.program_id(0) == 0)
    def _():
        sum_ref[...] = jnp.zeros_like(sum_ref)

    sum_ref[0:1, :dim] += jnp.sum(upstream * normed, axis=0, keepdims=True)
    sum_ref[1:2, :dim] += jnp.sum(upstream, axis=0, keepdims=True)
    sum_ref[2:3, :dim] += jnp.sum(grad, axis=0, keepdims=True)
    acc = jnp.zeros(part_ref.shape, F32)
    step = 512
    for k in range(w_up.shape[1] // step):
        span = slice(k * step, k * step + step)
        up = (dot(low, w_low[:, span]) * slope[:, span]).astype(BF16)
        up_ref[:, span] = up
        sum_ref[3:4, span] += jnp.sum(up.astype(F32), axis=0, keepdims=True)
        acc = acc + dot(up, w_up[:, span], ROW)
    part_ref[...] = acc.astype(BF16)


def branch_kernel(
    grad, mine, other, normed_ref, factor, att, gains, sums, w_back, first_ref, low_ref, dout_ref, delta_ref, sum_ref
):
    upstream = grad[...] + (mine[...].astype(F32) + other[...].astype(F32))
    normed = normed_ref[...]
    back = norm_back(upstream, normed, factor[:, :1], gains[0:1, :])
    first_ref[...] = back
    low = back.astype(BF16)
    low_ref[...] = low
    dim = low.shape[1]

    @pl.when(pl.program_id(0) == 0)
    def _():
        sum_ref[...] = sums[...]

    sum_ref[0:1, dim:] += jnp.sum(upstream * normed, axis=0, keepdims=True)
    sum_ref[1:2, dim:] += jnp.sum(upstream, axis=0, keepdims=True)
    sum_ref[2:3, dim:] += jnp.sum(back, axis=0, keepdims=True)
    dout = dot(low, w_back[...]).astype(BF16)
    dout_ref[...] = dout
    delta_ref[...] = jnp.zeros_like(delta_ref)
    for p in range(dout.shape[1] // 128):
        span = slice(p * 128, p * 128 + 128)
        turned = jnp.transpose(dout[:, span].astype(F32) * att[:, span].astype(F32))
        delta_ref[2 * p : 2 * p + 1, :] = jnp.sum(turned[:64], axis=0, keepdims=True)
        delta_ref[2 * p + 1 : 2 * p + 2, :] = jnp.sum(turned[64:], axis=0, keepdims=True)


def split(value):
    high = lax.reduce_precision(value, 8, 7)
    return high.astype(BF16), (value - high).astype(BF16)


def after(value, *others):
    return lax.optimization_barrier((value, others))[0]


def solution(mesh):
    n_fsdp, n_context = mesh.shape["fsdp"], mesh.shape["context"]
    direct_f, direct_c = n_fsdp == 4, n_context == 4
    swap = [(0, 1), (1, 0)]

    def partner(value, axis, d):
        return lax.ppermute(value, axis, [(i, i ^ d) for i in range(4)])

    def twin(value):
        return lax.ppermute(value, "tensor", swap)

    def pair_sum(value):
        low = value.astype(BF16)
        return low.astype(F32) + twin(low).astype(F32)

    def send_weight(shard, axis=0):
        if not direct_f:
            return [lax.all_gather(shard, "fsdp", axis=axis, tiled=True)]
        return [shard] + [partner(shard, "fsdp", d) for d in (1, 2, 3)]

    def weight_spots(pieces, axis=0):
        rows = pieces[0].shape[axis]
        if not direct_f:
            return [lambda s: (rows, 0)]
        return [lambda s, d=d: (rows, (s[6] ^ d) * rows) for d in range(4)]

    def send_rows(block, stats=None):
        if not direct_c:
            whole = lax.all_gather(block, "context", axis=0, tiled=True)
            if stats is None:
                return [whole]
            return [whole, lax.all_gather(stats, "context", axis=1, tiled=True)]
        half = block.shape[0] // 2
        mine = lax.dynamic_slice_in_dim(block, lax.axis_index("tensor") * half, half, 0)
        if stats is not None:
            mine = jnp.concatenate((mine,) + split(stats), axis=0)
        near = partner(mine, "context", 1)
        far = partner(mine, "context", 2)
        inner = lax.ppermute(mine, "context", [(1, 2), (2, 1)])
        return [near, far, inner]

    def row_pieces(block, got):
        if not direct_c:
            rows = got[0].shape[0]
            return got[:1], [lambda s: (rows, 0)]
        rows = block.shape[0]
        half = rows // 2
        pieces, spots = [block], [lambda s: (rows, s[4] * rows)]
        for d in (1, 2, 3):
            pieces.append(got[d - 1])
            spots.append(lambda s, d=d: (half, (s[4] ^ d) * rows + s[5] * half))
            pieces.append(twin(got[d - 1]))
            spots.append(lambda s, d=d: (half, (s[4] ^ d) * rows + (1 - s[5]) * half))
        return pieces, spots

    def row_stats(stats, got, half):
        if not direct_c:
            return got[1]
        both = [piece[half : half + 16].astype(F32) + piece[half + 16 :].astype(F32) for piece in got]
        return jnp.concatenate([stats] + both, axis=1)

    def pack(small, cols):
        high, low = split(small)
        filler = jnp.zeros((16 - 2 * small.shape[0], cols), BF16)
        return jnp.concatenate([high, low, filler], axis=0)

    def unpack(block, rows):
        return block[:rows].astype(F32) + block[rows : 2 * rows].astype(F32)

    def send_f(partials, small=None):
        if not direct_f:
            whole = jnp.concatenate(partials, axis=1)
            share = lax.psum_scatter(whole, "fsdp", scatter_dimension=0, tiled=True)
            return [share], None if small is None else lax.psum(small, "fsdp")
        me, rows = lax.axis_index("fsdp"), partials[0].shape[0] // 4
        cols = sum([partial.shape[1] for partial in partials])
        extra = [] if small is None else [pack(small, cols)]
        blocks = []
        for d in range(4):
            cut = [lax.dynamic_slice_in_dim(p, (me ^ d) * rows, rows, 0) for p in partials]
            piece = jnp.concatenate(cut, axis=1) if len(cut) > 1 else cut[0]
            if d:
                piece = jnp.concatenate([piece] + extra, axis=0) if extra else piece
                piece = partner(piece, "fsdp", d)
            blocks.append(piece)
        return blocks, small

    def finish_f(blocks, small=None):
        if not direct_f:
            return blocks[0], small
        rows = blocks[0].shape[0]
        parts = [block[:rows].astype(F32) for block in blocks]
        share = ((parts[0] + parts[1]) + (parts[2] + parts[3])).astype(BF16)
        if small is None:
            return share, None
        more = [unpack(block[rows:], small.shape[0]) for block in blocks[1:]]
        return share, (small + more[0]) + (more[1] + more[2])

    def send_z(mine, theirs, small, d):
        if small is not None:
            theirs = jnp.concatenate([theirs, pack(small, mine.shape[1])], axis=0)
        return (mine, partner(theirs, "context", d), small)

    def send_1(share, small=None):
        if not direct_c:
            return (share, small)
        side, rows = lax.rem(lax.axis_index("context"), 2), share.shape[0] // 2
        mine = lax.dynamic_slice_in_dim(share, side * rows, rows, 0)
        theirs = lax.dynamic_slice_in_dim(share, (1 - side) * rows, rows, 0)
        return send_z(mine, theirs, small, 1)

    def finish_z(state):
        if not direct_c:
            return state
        mine, got, small = state
        rows = mine.shape[0]
        total = (mine.astype(F32) + got[:rows].astype(F32)).astype(BF16)
        if small is not None:
            small = small + unpack(got[rows:], small.shape[0])
        return total, small

    def send_2(share, small=None):
        if not direct_c:
            return (share, small)
        return send_z(share, share, small, 2)

    def send_3(share, small=None):
        if not direct_c:
            total = lax.psum(share, "context")
            return (total, None if small is None else lax.psum(small, "context"))
        return (share, partner(share, "context", 1), small)

    def finish_3(state):
        if not direct_c:
            return state[0].astype(F32), state[1]
        share, other, small = state
        side = lax.rem(lax.axis_index("context"), 2)
        first = jnp.where(side == 0, share, other)
        second = jnp.where(side == 0, other, share)
        return jnp.concatenate([first, second], axis=0).astype(F32), small

    def shards(
        tokens,
        cotangent,
        w_qkv,
        bias_qv,
        w_attn_out,
        w_up,
        bias_up,
        w_down,
        gains,
        shifts,
        seq_lengths,
        key_mask,
    ):
        rows = tokens.shape[0]
        width = w_qkv.shape[2]
        pairs = width // 128
        hidden = w_up.shape[1]
        total = key_mask.shape[0]
        dim = tokens.shape[1]
        b1 = seq_lengths[0, 0]
        b2 = b1 + seq_lengths[0, 1]
        me = lax.axis_index("context")
        order = me if direct_c else 0 * me
        scalars = jnp.stack(
            [b1, b2, me * rows, order, me, lax.axis_index("tensor"), lax.axis_index("fsdp")]
        ).astype(jnp.int32)
        kb = jnp.where(key_mask == 1, 0.0, NEG).astype(F32).reshape(total // BK, 1, BK)

        got = send_rows(tokens)
        wq = send_weight(w_qkv, 1)
        got, wq = lax.optimization_barrier((got, wq))
        shard = jnp.concatenate([w_attn_out.T, w_up, w_down.T], axis=1)
        rest = send_weight(after(shard, wq[-1]))
        cuts = [(0, width), (width, hidden), (width + hidden, hidden)]
        zero = jnp.zeros((width,), F32)
        bias_row = jnp.concatenate([bias_qv[0], zero, bias_qv[1]]).reshape(1, -1)
        scale_row = jnp.concatenate([zero + 0.125 * LOG2E, zero + 1.0, zero + 1.0]).reshape(1, -1)
        pieces, spots = row_pieces(tokens, got)
        qkv, w_proj = project(
            scalars, pieces, spots, total, wq, weight_spots(wq, 1), bias_row, scale_row
        )
        attended, lset = attend(scalars, qkv, kb, rows, pairs)
        rest = after(rest, attended)
        w_back, w_upper, w_lower = place(scalars, rest, weight_spots(rest), dim, cuts)

        part = dot(attended, w_back, ROW).astype(BF16)
        work = 4 * rows * dim * hidden
        normed1, factor1, first_low, active, slope, part = call_rows(
            upper_kernel,
            rows,
            "upper",
            [tokens, part, twin(part)],
            [gains, shifts, bias_up.reshape(1, hidden), w_upper, w_lower],
            [(dim, F32), (128, F32), (dim, BF16), (hidden, BF16), (hidden, F32), (dim, BF16)],
            flops=2 * work,
        )
        out, grad_second, lower_grad, grad_upper, part, sums = call_rows(
            lower_kernel,
            rows,
            "lower",
            [normed1, part, twin(part), cotangent, slope],
            [gains, shifts, w_upper, w_lower],
            [(dim, BF16), (dim, F32), (dim, BF16), (hidden, BF16), (dim, BF16)],
            [hidden],
            flops=work,
        )
        other = twin(part)
        group_a, _ = send_f([dot(lower_grad.T, active).astype(BF16)])
        grad_first_sum, branch_grad, dout, deltat, small = call_rows(
            branch_kernel,
            rows,
            "branch",
            [grad_second, part, other, normed1, factor1, attended],
            [gains, sums, w_back],
            [(dim, F32), (dim, BF16), (width, BF16), (8, "turned")],
            [hidden],
            flops=work // 8,
        )
        stats = jnp.concatenate([lset, deltat], axis=0)
        got = send_rows(branch_grad, stats)
        group_b, small = send_f([dot(first_low.T, grad_upper).astype(BF16)], small)
        dq = query_grads(scalars, qkv, dout, stats, kb, rows, pairs)

        got = after(got, dq)
        stats_all = row_stats(stats, got, rows // 2)
        pieces, spots = row_pieces(branch_grad, got)
        (dout_all,) = project(scalars, pieces, spots, total, [w_back], None)
        group_a, _ = finish_f(after(group_a, dq))
        group_b, small = finish_f(after(group_b, dq), small)
        state_a, state_b = send_1(group_a), send_1(group_b, small)
        dks, dvs = [], []
        gate = (group_a, group_b)
        for pair in range(pairs):
            dk, dv = key_grads(
                after(scalars, gate), qkv, dout_all, stats_all, kb, rows, pairs, pair
            )
            dks.append(dk)
            dvs.append(dv)
            if pair == 0:
                group_a, group_b = finish_z(after(state_a, dk)), finish_z(after(state_b, dk))
                state_a, state_b = send_2(*group_a), send_2(*group_b)
                gate = (group_a, group_b)
            elif pair == 1:
                group_a, group_b = finish_z(after(state_a, dk)), finish_z(after(state_b, dk))
                state_a, state_b = send_3(*group_a), send_3(*group_b)
                early = jnp.concatenate([dq] + dks + dvs, axis=1)
                sums = jnp.sum(early.astype(F32), axis=0, keepdims=True)
                row = jnp.pad(sums, ((0, 0), (0, width)))
                group_c, row = send_f(
                    [
                        dot(tokens.T, early).astype(BF16),
                        dot(branch_grad.T, attended).astype(BF16),
                    ],
                    row,
                )
                gate = (group_a, group_b)
        late = jnp.concatenate([dks[-1], dvs[-1]], axis=1)
        tail = jnp.sum(late.astype(F32), axis=0, keepdims=True)
        group_d, tail = send_f([dot(tokens.T, late).astype(BF16)], tail)
        group_c, row = finish_f(after(group_c, late), row)
        state_c = send_1(group_c, row)
        stacked = jnp.concatenate([dq] + dks + dvs, axis=1)
        input_part = pair_sum(dot(stacked, w_proj, ROW))
        grad_tokens = (grad_first_sum + input_part).astype(BF16)
        group_d, tail = finish_f(group_d, tail)
        state_d = send_1(group_d, tail)
        state_c, state_d = send_2(*finish_z(state_c)), send_2(*finish_z(state_d))
        group_a, _ = finish_3(after(state_a, late))
        group_b, small = finish_3(after(state_b, late))
        state_c, state_d = send_3(*finish_z(state_c)), send_3(*finish_z(state_d))
        group_c, row = finish_3(state_c)
        group_d, tail = finish_3(state_d)

        sum_gains = jnp.stack([small[0, dim:], small[0, :dim]])
        sum_shifts = jnp.stack([small[2, dim:], small[1, dim:], small[2, :dim], small[1, :dim]])
        sum_bias_up = small[3]
        near_k = width + width - 128
        near_v = near_k + width - 128
        sum_bias_qv = jnp.stack(
            [row[0, :width], jnp.concatenate([row[0, near_k:near_v], tail[0, 128:]])]
        )
        share_qkv = jnp.stack(
            [
                group_c[:, :width],
                jnp.concatenate([group_c[:, width:near_k], group_d[:, :128]], axis=1),
                jnp.concatenate([group_c[:, near_k:near_v], group_d[:, 128:]], axis=1),
            ]
        )
        share_lower = group_a.T
        share_upper = group_b
        share_back = group_c[:, near_v:].T
        return (
            out,
            grad_tokens,
            share_qkv,
            share_back,
            share_upper,
            share_lower,
            sum_bias_qv,
            sum_bias_up,
            sum_gains,
            sum_shifts,
        )

    return jax.shard_map(
        shards,
        mesh=mesh,
        in_specs=(
            P(("fsdp", "context"), None),
            P(("fsdp", "context"), None),
            P(None, "fsdp", "tensor"),
            P(None, "tensor"),
            P("tensor", "fsdp"),
            P("fsdp", "tensor"),
            P("tensor"),
            P("tensor", "fsdp"),
            P(),
            P(),
            P("fsdp", None),
            P("fsdp"),
        ),
        out_specs=(
            P(("fsdp", "context"), None),
            P(("fsdp", "context"), None),
            P(None, "fsdp", "tensor"),
            P("tensor", "fsdp"),
            P("fsdp", "tensor"),
            P("tensor", "fsdp"),
            P(None, "tensor"),
            P("tensor"),
            P(),
            P(),
        ),
        check_vma=False,
    )
```

```python
import jax
import jax.numpy as jnp
import numpy as np
from jax import lax
from jax.experimental import pallas as pl
from jax.experimental.pallas import tpu as pltpu
from jax.sharding import PartitionSpec as P

EPSILON = 1e-12
LOG2E = 1.4426950408889634
NEG = -1e30
BQ = 256
BK = 256
F32 = jnp.float32
BF16 = jnp.bfloat16
ROW = (((1,), (1,)), ((), ()))
COL = (((1,), (0,)), ((), ()))
LIMIT = 56 * 1024 * 1024
COST = pl.CostEstimate(flops=36_000_000_000, transcendentals=0, bytes_accessed=8_000_000)
PAIR_COST = pl.CostEstimate(flops=14_000_000_000, transcendentals=0, bytes_accessed=4_000_000)


def dot(a, b, dims=COL):
    return lax.dot_general(a, b, dims, preferred_element_type=F32)


def normalize(inputs):
    center = inputs - jnp.mean(inputs, axis=-1, keepdims=True)
    factor = lax.rsqrt(jnp.mean(center * center, axis=-1, keepdims=True) + EPSILON)
    return (center * factor, factor)


def norm_back(upstream, normed, factor, gain):
    scaled = upstream * gain
    return factor * (
        scaled
        - jnp.mean(scaled, axis=-1, keepdims=True)
        - normed * jnp.mean(scaled * normed, axis=-1, keepdims=True)
    )


def segment_of(places, b1, b2):
    return (places >= b1).astype(jnp.int32) + (places >= b2).astype(jnp.int32)


def key_range(first, last, b1, b2, total):
    lo = jnp.where(first >= b2, b2, jnp.where(first >= b1, b1, 0))
    hi = jnp.where(last >= b2, total, jnp.where(last >= b1, b2, b1))
    return lo, hi


def half_mask(rows, side):
    lane = lax.broadcasted_iota(jnp.int32, (rows, 128), 1)
    return (lane < 64) if side == 0 else (lane >= 64)


def pick(pair, side):
    return jnp.where(half_mask(pair.shape[0], side), pair, jnp.zeros_like(pair))


def column(row):
    return jnp.transpose(jnp.broadcast_to(row, (128, row.shape[1])))[:, :1]


def fill_bias(bias_ref, kb_ref, first, b1, b2, j0, j1):
    cols = first + lax.broadcasted_iota(jnp.int32, (1, BQ), 1)
    col_seg = segment_of(cols, b1, b2)

    def body(j, carry):
        rows = j * BK + lax.broadcasted_iota(jnp.int32, (BK, 1), 0)
        row_seg = segment_of(rows, b1, b2)
        kept = jnp.where(rows == cols, 0.0, jnp.broadcast_to(column(kb_ref[j]), (BK, BQ)))
        bias_ref[j] = jnp.where(row_seg == col_seg, kept, NEG)
        return carry

    lax.fori_loop(j0, j1, body, 0)


def attend_kernel(s_ref, q_ref, k_ref, v_ref, kb_ref, o_ref, lset_ref, score, bias):
    total = k_ref.shape[0]
    pairs = q_ref.shape[1] // 128
    b1, b2 = s_ref[0], s_ref[1]
    first = s_ref[2] + pl.program_id(0) * BQ
    lo, hi = key_range(first, first + BQ - 1, b1, b2, total)
    j0, j1 = lo // BK, (hi + BK - 1) // BK
    fill_bias(bias, kb_ref, first, b1, b2, j0, j1)
    peaks = None
    for p in range(-1, pairs):
        nxt = p + 1
        if nxt < pairs:
            ahead = slice(nxt * 128, nxt * 128 + 128)
            heads = [jnp.transpose(pick(q_ref[:, ahead], side)) for side in range(2)]
        here = slice(p * 128, p * 128 + 128)

        def body(j, carry):
            tops, tots, accs = [list(part) for part in carry]
            rows = pl.ds(pl.multiple_of(j * BK, BK), BK)
            if nxt < pairs:
                keys = k_ref[rows, ahead]
                for side in range(2):
                    s = dot(keys, heads[side]) + bias[j]
                    score[nxt % 2, side, j] = s
                    tops[side] = jnp.maximum(tops[side], jnp.max(s.reshape(BK // 8, 8, BQ), axis=0))
            if p >= 0:
                turned = jnp.transpose(v_ref[rows, here])
                for side in range(2):
                    prob = jnp.exp2(score[p % 2, side, j] - peaks[side])
                    tots[side] = tots[side] + jnp.sum(prob.reshape(BK // 8, 8, BQ), axis=0)
                    accs[side] = accs[side] + dot(
                        turned[64 * side : 64 * side + 64], prob.astype(BF16)
                    )
            return (tuple(tops), tuple(tots), tuple(accs))

        low, zero, wide = jnp.full((8, BQ), NEG, F32), jnp.zeros((8, BQ), F32), jnp.zeros((64, BQ), F32)
        tops, tots, accs = lax.fori_loop(j0, j1, body, ((low, low), (zero, zero), (wide, wide)))
        if p >= 0:
            results = []
            for side in range(2):
                h = 2 * p + side
                whole = jnp.sum(tots[side], axis=0, keepdims=True)
                results.append(accs[side] * (1.0 / whole))
                lset_ref[h : h + 1, :] = peaks[side] + jnp.log2(whole)
            o_ref[:, here] = jnp.transpose(jnp.concatenate(results, axis=0)).astype(BF16)
        peaks = [jnp.max(top, axis=0, keepdims=True) for top in tops]


def attend(scalars, qkv, kb, rows, pairs):
    total = qkv.shape[0]
    width = pairs * 128
    return pl.pallas_call(
        attend_kernel,
        grid_spec=pltpu.PrefetchScalarGridSpec(
            num_scalar_prefetch=1,
            grid=(rows // BQ,),
            in_specs=[
                pl.BlockSpec((BQ, width), lambda i, s: (s[2] // BQ + i, 0)),
                pl.BlockSpec((total, width), lambda i, s: (0, 1), pipeline_mode=pl.Buffered(1)),
                pl.BlockSpec((total, width), lambda i, s: (0, 2), pipeline_mode=pl.Buffered(1)),
                pl.BlockSpec((total // BK, 1, BK), lambda i, s: (0, 0, 0)),
            ],
            out_specs=[
                pl.BlockSpec((BQ, width), lambda i, s: (i, 0)),
                pl.BlockSpec((8, BQ), lambda i, s: (0, i)),
            ],
            scratch_shapes=[
                pltpu.VMEM((2, 2, total // BK, BK, BQ), F32),
                pltpu.VMEM((total // BK, BK, BQ), F32),
            ],
        ),
        out_shape=[
            jax.ShapeDtypeStruct((rows, width), BF16),
            jax.ShapeDtypeStruct((8, rows), F32),
        ],
        compiler_params=pltpu.CompilerParams(
            dimension_semantics=("arbitrary",), vmem_limit_bytes=LIMIT
        ),
        cost_estimate=COST,
        name="attend",
    )(scalars, qkv, qkv, qkv, kb)


def query_kernel(s_ref, q_ref, k_ref, v_ref, do_ref, stat_ref, kb_ref, dq_ref, bias):
    total = k_ref.shape[0]
    pairs = q_ref.shape[1] // 128
    b1, b2 = s_ref[0], s_ref[1]
    first = s_ref[2] + pl.program_id(0) * BQ
    lo, hi = key_range(first, first + BQ - 1, b1, b2, total)
    j0, j1 = lo // BK, (hi + BK - 1) // BK
    fill_bias(bias, kb_ref, first, b1, b2, j0, j1)
    for p in range(pairs):
        span = slice(p * 128, p * 128 + 128)
        sides = []
        for side in range(2):
            h = 2 * p + side
            sides.append(
                (
                    jnp.transpose(pick(q_ref[:, span], side)),
                    jnp.transpose(pick(do_ref[:, span], side)),
                    stat_ref[8 + h : 9 + h, :],
                    stat_ref[h : h + 1, :],
                )
            )

        def body(j, accs):
            rows = pl.ds(pl.multiple_of(j * BK, BK), BK)
            keys = k_ref[rows, span]
            values = v_ref[rows, span]
            turned = jnp.transpose(keys)
            out = []
            for side in range(2):
                qh, gh, delta, lse = sides[side]
                prob = jnp.exp2(dot(keys, qh) + bias[j] - lse)
                score = (prob * (dot(values, gh) - delta)).astype(BF16)
                out.append(accs[side] + dot(turned[64 * side : 64 * side + 64], score))
            return tuple(out)

        zero = jnp.zeros((64, BQ), F32)
        both = lax.fori_loop(j0, j1, body, (zero, zero))
        dq_ref[:, span] = (jnp.transpose(jnp.concatenate(both, axis=0)) * 0.125).astype(BF16)


def query_grads(scalars, qkv, dout, stats, kb, rows, pairs):
    total = qkv.shape[0]
    width = pairs * 128
    return pl.pallas_call(
        query_kernel,
        grid_spec=pltpu.PrefetchScalarGridSpec(
            num_scalar_prefetch=1,
            grid=(rows // BQ,),
            in_specs=[
                pl.BlockSpec((BQ, width), lambda i, s: (s[2] // BQ + i, 0)),
                pl.BlockSpec((total, width), lambda i, s: (0, 1), pipeline_mode=pl.Buffered(1)),
                pl.BlockSpec((total, width), lambda i, s: (0, 2), pipeline_mode=pl.Buffered(1)),
                pl.BlockSpec((BQ, width), lambda i, s: (i, 0)),
                pl.BlockSpec((16, BQ), lambda i, s: (0, i)),
                pl.BlockSpec((total // BK, 1, BK), lambda i, s: (0, 0, 0)),
            ],
            out_specs=pl.BlockSpec((BQ, width), lambda i, s: (i, 0)),
            scratch_shapes=[pltpu.VMEM((total // BK, BK, BQ), F32)],
        ),
        out_shape=jax.ShapeDtypeStruct((rows, width), BF16),
        compiler_params=pltpu.CompilerParams(
            dimension_semantics=("arbitrary",), vmem_limit_bytes=LIMIT
        ),
        cost_estimate=COST,
        name="query_grads",
    )(scalars, qkv, qkv, qkv, dout, stats, kb)


def key_kernel(s_ref, k_ref, v_ref, q_ref, do_ref, stat_ref, mask_ref, dk_ref, dv_ref, *, pair, per):
    total = q_ref.shape[0]
    b1, b2 = s_ref[0], s_ref[1]
    first = s_ref[2] + pl.program_id(0) * BK
    lo, hi = key_range(first, first + BK - 1, b1, b2, total)
    j0, j1 = lo // BQ, (hi + BQ - 1) // BQ
    cols = first + lax.broadcasted_iota(jnp.int32, (1, BK), 1)
    col_seg = segment_of(cols, b1, b2)
    masked = jnp.broadcast_to(mask_ref[0], (BQ, BK))
    sides = [
        (jnp.transpose(pick(k_ref[...], side)), jnp.transpose(pick(v_ref[...], side)))
        for side in range(2)
    ]

    def body(j, carry):
        span = pl.ds(pl.multiple_of(j * BQ, BQ), BQ)
        rows = j * BQ + lax.broadcasted_iota(jnp.int32, (BQ, 1), 0)
        row_seg = segment_of(rows, b1, b2)
        bias = jnp.where(row_seg == col_seg, jnp.where(rows == cols, 0.0, masked), NEG)
        queries, grads = q_ref[span, :], do_ref[span, :]
        qt, gt = jnp.transpose(queries), jnp.transpose(grads)
        place = ((j // per) ^ s_ref[3]) * per + lax.rem(j, per)
        stats = jnp.transpose(stat_ref[:, pl.ds(pl.multiple_of(place * BQ, BQ), BQ)])
        out = []
        for side in range(2):
            h = 2 * pair + side
            kh, vh = sides[side]
            part = slice(64 * side, 64 * side + 64)
            dk, dv = carry[side]
            prob = jnp.exp2(dot(queries, kh) + bias - stats[:, h : h + 1])
            score = prob * (dot(grads, vh) - stats[:, 8 + h : 9 + h])
            out.append(
                (dk + dot(qt[part], score.astype(BF16)), dv + dot(gt[part], prob.astype(BF16)))
            )
        return tuple(out)

    zero = jnp.zeros((64, BK), F32)
    (k0, v0), (k1, v1) = lax.fori_loop(j0, j1, body, ((zero, zero), (zero, zero)))
    dk_ref[...] = (jnp.transpose(jnp.concatenate([k0, k1], axis=0)) * (1.0 / LOG2E)).astype(BF16)
    dv_ref[...] = jnp.transpose(jnp.concatenate([v0, v1], axis=0)).astype(BF16)


def key_grads(scalars, qkv, dout, stats, kb, rows, pairs, pair):
    total = qkv.shape[0]

    def kernel(*refs):
        key_kernel(*refs, pair=pair, per=rows // BQ)

    return pl.pallas_call(
        kernel,
        grid_spec=pltpu.PrefetchScalarGridSpec(
            num_scalar_prefetch=1,
            grid=(rows // BK,),
            in_specs=[
                pl.BlockSpec((BK, 128), lambda i, s: (s[2] // BK + i, pairs + pair)),
                pl.BlockSpec((BK, 128), lambda i, s: (s[2] // BK + i, 2 * pairs + pair)),
                pl.BlockSpec((total, 128), lambda i, s: (0, pair), pipeline_mode=pl.Buffered(1)),
                pl.BlockSpec((total, 128), lambda i, s: (0, pair), pipeline_mode=pl.Buffered(1)),
                pl.BlockSpec((16, total), lambda i, s: (0, 0), pipeline_mode=pl.Buffered(1)),
                pl.BlockSpec((1, 1, BK), lambda i, s: (s[2] // BK + i, 0, 0)),
            ],
            out_specs=[
                pl.BlockSpec((BK, 128), lambda i, s: (i, 0)),
                pl.BlockSpec((BK, 128), lambda i, s: (i, 0)),
            ],
        ),
        out_shape=[jax.ShapeDtypeStruct((rows, 128), BF16)] * 2,
        compiler_params=pltpu.CompilerParams(
            dimension_semantics=("arbitrary",), vmem_limit_bytes=LIMIT
        ),
        cost_estimate=PAIR_COST,
        name="key_grads",
    )(scalars, qkv, qkv, qkv, dout, stats, kb)


def put(out_ref, piece, height, start, low=0):
    unit = 192 if height % 192 == 0 else 16
    span = pl.ds(pl.multiple_of(start, unit), height)
    if len(piece.shape) == 3:
        wide = piece.shape[2]
        for k in range(piece.shape[0]):
            out_ref[span, k * wide : (k + 1) * wide] = piece[k]
    else:
        wide = out_ref.shape[1]
        out_ref[span, :] = piece[:height, low : low + wide]


def whole_spec(value):
    zeros = (0,) * value.ndim
    return pl.BlockSpec(value.shape, lambda i, s: zeros, pipeline_mode=pl.Buffered(1))


def place(scalars, pieces, spots, total, cuts):
    count = len(pieces)

    def kernel(s_ref, *refs):
        for i in range(count):
            height, start = spots[i](s_ref)
            for k, (low, wide) in enumerate(cuts):
                put(refs[count + k], refs[i], height, start, low)

    return pl.pallas_call(
        kernel,
        grid_spec=pltpu.PrefetchScalarGridSpec(
            num_scalar_prefetch=1,
            grid=(1,),
            in_specs=[whole_spec(piece) for piece in pieces],
            out_specs=[pl.BlockSpec((total, wide), lambda i, s: (0, 0)) for _, wide in cuts],
        ),
        out_shape=[jax.ShapeDtypeStruct((total, wide), BF16) for _, wide in cuts],
        compiler_params=pltpu.CompilerParams(vmem_limit_bytes=LIMIT),
        name="place",
    )(scalars, *pieces)


def project(scalars, pieces, spots, total, weights, wspots, bias=None, scale=None):
    count, wcount = len(pieces), len(weights)
    depth = pieces[0].shape[1]
    last = weights[0]
    cols = last.shape[1] if last.ndim == 2 else last.shape[0] * last.shape[2]
    block = 512
    extra = [] if bias is None else [bias, scale]
    keep = bias is not None

    def kernel(s_ref, *refs):
        ins, ws = refs[:count], refs[count : count + wcount]
        rest = refs[count + wcount :]
        if keep:
            bias_ref, scale_ref, out_ref, w_ref, x_ref = rest
        else:
            out_ref, x_ref = rest
            w_ref = ws[0]
        step = pl.program_id(0)

        @pl.when(step == 0)
        def _():
            for i in range(count):
                height, start = spots[i](s_ref)
                put(x_ref, ins[i], height, start)
            if keep:
                for i in range(wcount):
                    height, start = wspots[i](s_ref)
                    put(w_ref, ws[i], height, start)

        span = pl.ds(pl.multiple_of(step * block, block), block)
        value = dot(x_ref[span, :], w_ref[...])
        if keep:
            value = (value + bias_ref[...]) * scale_ref[...]
        out_ref[...] = value.astype(BF16)

    out_specs = [pl.BlockSpec((block, cols), lambda i, s: (i, 0))]
    out_shape = [jax.ShapeDtypeStruct((total, cols), BF16)]
    if keep:
        out_specs.append(pl.BlockSpec((depth, cols), lambda i, s: (0, 0)))
        out_shape.append(jax.ShapeDtypeStruct((depth, cols), BF16))
    return pl.pallas_call(
        kernel,
        grid_spec=pltpu.PrefetchScalarGridSpec(
            num_scalar_prefetch=1,
            grid=(total // block,),
            in_specs=[whole_spec(piece) for piece in pieces + weights + extra],
            out_specs=out_specs,
            scratch_shapes=[pltpu.VMEM((total, depth), BF16)],
        ),
        out_shape=out_shape,
        compiler_params=pltpu.CompilerParams(
            dimension_semantics=("arbitrary",), vmem_limit_bytes=LIMIT
        ),
        cost_estimate=pl.CostEstimate(
            flops=2 * total * depth * cols, transcendentals=0, bytes_accessed=4_000_000
        ),
        name="project",
    )(scalars, *pieces, *weights, *extra)


def project_slots(scalars, slots, weights, wspots, bias, scale, total, whole=None):
    rows, depth = slots[0][1][0].shape[0] * len(slots[0][1]), slots[0][1][0].shape[1]
    pieces = [piece for _, group in slots for piece in group]
    count, wcount = len(pieces), len(weights)
    cols = bias.shape[1]
    fresh = whole is None
    offsets = [d for d, _ in slots]

    def kernel(s_ref, *refs):
        ins, ws = refs[:count], refs[count : count + wcount]
        bias_ref, scale_ref = refs[count + wcount : count + wcount + 2]
        rest = refs[count + wcount + 2 :]
        if fresh:
            out_ref, w_ref, x_ref = rest
        else:
            _, out_ref, x_ref = rest
            w_ref = ws[0]
        step = pl.program_id(0)
        if fresh:

            @pl.when(step == 0)
            def _():
                for i in range(wcount):
                    height, start = wspots[i](s_ref)
                    put(w_ref, ws[i], height, start)

        seen = 0
        for k, (_, group) in enumerate(slots):
            own = ins[seen : seen + len(group)]
            seen += len(group)

            @pl.when(step == k)
            def _(own=own):
                if len(own) == 1:
                    x_ref[...] = own[0][...]
                else:
                    half = rows // 2
                    put(x_ref, own[0], half, s_ref[5] * half)
                    put(x_ref, own[1], half, (1 - s_ref[5]) * half)

        value = (dot(x_ref[...], w_ref[...]) + bias_ref[...]) * scale_ref[...]
        out_ref[...] = value.astype(BF16)

    def spot(i, s):
        d = offsets[0]
        for k in range(1, len(offsets)):
            d = jnp.where(i == k, offsets[k], d)
        return (s[4] ^ d, 0)

    operands = pieces + weights + [bias, scale]
    in_specs = [whole_spec(value) for value in operands]
    out_specs = [pl.BlockSpec((rows, cols), spot)]
    out_shape = [jax.ShapeDtypeStruct((total, cols), BF16)]
    aliases = {}
    if fresh:
        out_specs.append(pl.BlockSpec((depth, cols), lambda i, s: (0, 0)))
        out_shape.append(jax.ShapeDtypeStruct((depth, cols), BF16))
    else:
        aliases = {1 + len(operands): 0}
        operands = operands + [whole]
        in_specs.append(pl.BlockSpec(memory_space=pl.ANY))
    return pl.pallas_call(
        kernel,
        grid_spec=pltpu.PrefetchScalarGridSpec(
            num_scalar_prefetch=1,
            grid=(len(slots),),
            in_specs=in_specs,
            out_specs=out_specs,
            scratch_shapes=[pltpu.VMEM((rows, depth), BF16)],
        ),
        out_shape=out_shape,
        input_output_aliases=aliases,
        compiler_params=pltpu.CompilerParams(
            dimension_semantics=("arbitrary",), vmem_limit_bytes=LIMIT
        ),
        cost_estimate=pl.CostEstimate(
            flops=2 * len(slots) * rows * depth * cols, transcendentals=0, bytes_accessed=4_000_000
        ),
        name="project_slots",
    )(scalars, *operands)


def call_rows(kernel, rows, name, blocked, fixed, outs, kept=(), flops=0):
    specs = [pl.BlockSpec((BQ,) + v.shape[1:], lambda i: (i, 0)) for v in blocked]
    specs += [pl.BlockSpec(v.shape, lambda i: (0, 0), pipeline_mode=pl.Buffered(1)) for v in fixed]
    shapes, out_specs = [], []
    for wide, kind in outs:
        if kind == "turned":
            shapes.append(jax.ShapeDtypeStruct((8, rows), F32))
            out_specs.append(pl.BlockSpec((8, BQ), lambda i: (0, i)))
        else:
            shapes.append(jax.ShapeDtypeStruct((rows, wide), kind))
            out_specs.append(pl.BlockSpec((BQ, wide), lambda i: (i, 0)))
    for wide in kept:
        shapes.append(jax.ShapeDtypeStruct((8, wide), F32))
        out_specs.append(pl.BlockSpec((8, wide), lambda i: (0, 0)))
    return pl.pallas_call(
        kernel,
        grid=(rows // BQ,),
        in_specs=specs,
        out_specs=out_specs,
        out_shape=shapes,
        compiler_params=pltpu.CompilerParams(
            dimension_semantics=("arbitrary",), vmem_limit_bytes=LIMIT
        ),
        cost_estimate=pl.CostEstimate(flops=flops, transcendentals=0, bytes_accessed=4_000_000),
        name=name,
    )(*blocked, *fixed)


def upper_kernel(
    tok, mine, other, gains, shifts, bias, w_up, w_low, normed_ref, factor_ref, low_ref, active_ref, slope_ref, part_ref
):
    total = tok[...].astype(F32) + (mine[...].astype(F32) + other[...].astype(F32)) + shifts[0:1, :]
    normed, factor = normalize(total)
    normed_ref[...] = normed
    factor_ref[...] = jnp.broadcast_to(factor, factor_ref.shape)
    low = (normed * gains[0:1, :] + shifts[1:2, :]).astype(BF16)
    low_ref[...] = low
    acc = jnp.zeros(part_ref.shape, F32)
    step = 512
    for k in range(w_up.shape[1] // step):
        span = slice(k * step, k * step + step)
        upper = dot(low, w_up[:, span]) + bias[:, span]
        half = 0.5 + 0.5 * lax.erf(upper * 0.7071067811865476)
        bell = jnp.exp2(upper * upper * (-0.5 * LOG2E)) * 0.3989422804014327
        slope_ref[:, span] = half + upper * bell
        active = (upper * half).astype(BF16)
        active_ref[:, span] = active
        acc = acc + dot(active, w_low[:, span], ROW)
    part_ref[...] = acc.astype(BF16)


def lower_kernel(
    normed_ref, mine, other, cot, slope, gains, shifts, w_up, w_low, out_ref, grad_ref, low_ref, up_ref, part_ref, sum_ref
):
    first = normed_ref[...] * gains[0:1, :] + shifts[1:2, :]
    total = first + (mine[...].astype(F32) + other[...].astype(F32)) + shifts[2:3, :]
    normed, factor = normalize(total)
    out_ref[...] = (normed * gains[1:2, :] + shifts[3:4, :]).astype(BF16)
    upstream = cot[...].astype(F32)
    grad = norm_back(upstream, normed, factor, gains[1:2, :])
    grad_ref[...] = grad
    low = grad.astype(BF16)
    low_ref[...] = low
    dim = low.shape[1]

    @pl.when(pl.program_id(0) == 0)
    def _():
        sum_ref[...] = jnp.zeros_like(sum_ref)

    sum_ref[0:1, :dim] += jnp.sum(upstream * normed, axis=0, keepdims=True)
    sum_ref[1:2, :dim] += jnp.sum(upstream, axis=0, keepdims=True)
    sum_ref[2:3, :dim] += jnp.sum(grad, axis=0, keepdims=True)
    acc = jnp.zeros(part_ref.shape, F32)
    step = 512
    for k in range(w_up.shape[1] // step):
        span = slice(k * step, k * step + step)
        up = (dot(low, w_low[:, span]) * slope[:, span]).astype(BF16)
        up_ref[:, span] = up
        sum_ref[3:4, span] += jnp.sum(up.astype(F32), axis=0, keepdims=True)
        acc = acc + dot(up, w_up[:, span], ROW)
    part_ref[...] = acc.astype(BF16)


def branch_kernel(
    grad, mine, other, normed_ref, factor, att, gains, sums, w_back, first_ref, low_ref, dout_ref, delta_ref, sum_ref
):
    upstream = grad[...] + (mine[...].astype(F32) + other[...].astype(F32))
    normed = normed_ref[...]
    back = norm_back(upstream, normed, factor[:, :1], gains[0:1, :])
    first_ref[...] = back
    low = back.astype(BF16)
    low_ref[...] = low
    dim = low.shape[1]

    @pl.when(pl.program_id(0) == 0)
    def _():
        sum_ref[...] = sums[...]

    sum_ref[0:1, dim:] += jnp.sum(upstream * normed, axis=0, keepdims=True)
    sum_ref[1:2, dim:] += jnp.sum(upstream, axis=0, keepdims=True)
    sum_ref[2:3, dim:] += jnp.sum(back, axis=0, keepdims=True)
    dout = dot(low, w_back[...]).astype(BF16)
    dout_ref[...] = dout
    delta_ref[...] = jnp.zeros_like(delta_ref)
    for p in range(dout.shape[1] // 128):
        span = slice(p * 128, p * 128 + 128)
        turned = jnp.transpose(dout[:, span].astype(F32) * att[:, span].astype(F32))
        delta_ref[2 * p : 2 * p + 1, :] = jnp.sum(turned[:64], axis=0, keepdims=True)
        delta_ref[2 * p + 1 : 2 * p + 2, :] = jnp.sum(turned[64:], axis=0, keepdims=True)


def split(value):
    high = lax.reduce_precision(value, 8, 7)
    return high.astype(BF16), (value - high).astype(BF16)


def after(value, *others):
    return lax.optimization_barrier((value, others))[0]


def solution(mesh):
    n_fsdp, n_context = mesh.shape["fsdp"], mesh.shape["context"]
    direct_f, direct_c = n_fsdp == 4, n_context == 4
    swap = [(0, 1), (1, 0)]

    def partner(value, axis, d):
        return lax.ppermute(value, axis, [(i, i ^ d) for i in range(4)])

    def twin(value):
        return lax.ppermute(value, "tensor", swap)

    def pair_sum(value):
        low = value.astype(BF16)
        return low.astype(F32) + twin(low).astype(F32)

    def send_weight(shard, axis=0):
        if not direct_f:
            return [lax.all_gather(shard, "fsdp", axis=axis, tiled=True)]
        return [shard] + [partner(shard, "fsdp", d) for d in (1, 2, 3)]

    def weight_spots(pieces, axis=0):
        rows = pieces[0].shape[axis]
        if not direct_f:
            return [lambda s: (rows, 0)]
        return [lambda s, d=d: (rows, (s[6] ^ d) * rows) for d in range(4)]

    def send_rows(block, stats=None):
        if not direct_c:
            whole = lax.all_gather(block, "context", axis=0, tiled=True)
            if stats is None:
                return [whole]
            return [whole, lax.all_gather(stats, "context", axis=1, tiled=True)]
        half = block.shape[0] // 2
        mine = lax.dynamic_slice_in_dim(block, lax.axis_index("tensor") * half, half, 0)
        if stats is not None:
            mine = jnp.concatenate((mine,) + split(stats), axis=0)
        near = partner(mine, "context", 1)
        far = partner(mine, "context", 2)
        inner = lax.ppermute(mine, "context", [(1, 2), (2, 1)])
        return [near, far, inner]

    def row_pieces(block, got):
        if not direct_c:
            rows = got[0].shape[0]
            return got[:1], [lambda s: (rows, 0)]
        rows = block.shape[0]
        half = rows // 2
        pieces, spots = [block], [lambda s: (rows, s[4] * rows)]
        for d in (1, 2, 3):
            pieces.append(got[d - 1])
            spots.append(lambda s, d=d: (half, (s[4] ^ d) * rows + s[5] * half))
            pieces.append(twin(got[d - 1]))
            spots.append(lambda s, d=d: (half, (s[4] ^ d) * rows + (1 - s[5]) * half))
        return pieces, spots

    def row_stats(stats, got, half):
        if not direct_c:
            return got[1]
        both = [piece[half : half + 16].astype(F32) + piece[half + 16 :].astype(F32) for piece in got]
        return jnp.concatenate([stats] + both, axis=1)

    def pack(small, cols):
        high, low = split(small)
        filler = jnp.zeros((16 - 2 * small.shape[0], cols), BF16)
        return jnp.concatenate([high, low, filler], axis=0)

    def unpack(block, rows):
        return block[:rows].astype(F32) + block[rows : 2 * rows].astype(F32)

    def send_f(partials, small=None):
        if not direct_f:
            whole = jnp.concatenate(partials, axis=1)
            share = lax.psum_scatter(whole, "fsdp", scatter_dimension=0, tiled=True)
            return [share], None if small is None else lax.psum(small, "fsdp")
        me, rows = lax.axis_index("fsdp"), partials[0].shape[0] // 4
        cols = sum([partial.shape[1] for partial in partials])
        extra = [] if small is None else [pack(small, cols)]
        blocks = []
        for d in range(4):
            cut = [lax.dynamic_slice_in_dim(p, (me ^ d) * rows, rows, 0) for p in partials]
            piece = jnp.concatenate(cut, axis=1) if len(cut) > 1 else cut[0]
            if d:
                piece = jnp.concatenate([piece] + extra, axis=0) if extra else piece
                piece = partner(piece, "fsdp", d)
            blocks.append(piece)
        return blocks, small

    def finish_f(blocks, small=None):
        if not direct_f:
            return blocks[0], small
        rows = blocks[0].shape[0]
        parts = [block[:rows].astype(F32) for block in blocks]
        share = ((parts[0] + parts[1]) + (parts[2] + parts[3])).astype(BF16)
        if small is None:
            return share, None
        more = [unpack(block[rows:], small.shape[0]) for block in blocks[1:]]
        return share, (small + more[0]) + (more[1] + more[2])

    def send_z(mine, theirs, small, d):
        if small is not None:
            theirs = jnp.concatenate([theirs, pack(small, mine.shape[1])], axis=0)
        return (mine, partner(theirs, "context", d), small)

    def send_1(share, small=None):
        if not direct_c:
            return (share, small)
        side, rows = lax.rem(lax.axis_index("context"), 2), share.shape[0] // 2
        mine = lax.dynamic_slice_in_dim(share, side * rows, rows, 0)
        theirs = lax.dynamic_slice_in_dim(share, (1 - side) * rows, rows, 0)
        return send_z(mine, theirs, small, 1)

    def finish_z(state):
        if not direct_c:
            return state
        mine, got, small = state
        rows = mine.shape[0]
        total = (mine.astype(F32) + got[:rows].astype(F32)).astype(BF16)
        if small is not None:
            small = small + unpack(got[rows:], small.shape[0])
        return total, small

    def send_2(share, small=None):
        if not direct_c:
            return (share, small)
        return send_z(share, share, small, 2)

    def send_3(share, small=None):
        if not direct_c:
            total = lax.psum(share, "context")
            return (total, None if small is None else lax.psum(small, "context"))
        return (share, partner(share, "context", 1), small)

    def finish_3(state):
        if not direct_c:
            return state[0].astype(F32), state[1]
        share, other, small = state
        side = lax.rem(lax.axis_index("context"), 2)
        first = jnp.where(side == 0, share, other)
        second = jnp.where(side == 0, other, share)
        return jnp.concatenate([first, second], axis=0).astype(F32), small

    def shards(
        tokens,
        cotangent,
        w_qkv,
        bias_qv,
        w_attn_out,
        w_up,
        bias_up,
        w_down,
        gains,
        shifts,
        seq_lengths,
        key_mask,
    ):
        rows = tokens.shape[0]
        width = w_qkv.shape[2]
        pairs = width // 128
        hidden = w_up.shape[1]
        total = key_mask.shape[0]
        dim = tokens.shape[1]
        b1 = seq_lengths[0, 0]
        b2 = b1 + seq_lengths[0, 1]
        me = lax.axis_index("context")
        order = me if direct_c else 0 * me
        scalars = jnp.stack(
            [b1, b2, me * rows, order, me, lax.axis_index("tensor"), lax.axis_index("fsdp")]
        ).astype(jnp.int32)
        kb = jnp.where(key_mask == 1, 0.0, NEG).astype(F32).reshape(total // BK, 1, BK)

        got = send_rows(tokens)
        wq = send_weight(w_qkv, 1)
        shard = jnp.concatenate([w_attn_out.T, w_up, w_down.T], axis=1)
        rest = send_weight(after(shard, wq[min(1, len(wq) - 1)]))
        cuts = [(0, width), (width, hidden), (width + hidden, hidden)]
        zero = jnp.zeros((width,), F32)
        bias_row = jnp.concatenate([bias_qv[0], zero, bias_qv[1]]).reshape(1, -1)
        scale_row = jnp.concatenate([zero + 0.125 * LOG2E, zero + 1.0, zero + 1.0]).reshape(1, -1)
        if direct_c:
            near, far, inner = got
            (near, inner), wq = lax.optimization_barrier(((near, inner), wq))
            slots = [(0, [tokens]), (1, [near, twin(near)]), (3, [inner, twin(inner)])]
            qkv, w_proj = project_slots(
                scalars, slots, wq, weight_spots(wq, 1), bias_row, scale_row, total
            )
            far = after(far, w_proj)
            (qkv,) = project_slots(
                scalars, [(2, [far, twin(far)])], [w_proj], None, bias_row, scale_row, total, qkv
            )
        else:
            pieces, spots = row_pieces(tokens, got)
            qkv, w_proj = project(
                scalars, pieces, spots, total, wq, weight_spots(wq, 1), bias_row, scale_row
            )
        attended, lset = attend(scalars, qkv, kb, rows, pairs)
        rest = after(rest, attended)
        w_back, w_upper, w_lower = place(scalars, rest, weight_spots(rest), dim, cuts)

        part = dot(attended, w_back, ROW).astype(BF16)
        work = 4 * rows * dim * hidden
        normed1, factor1, first_low, active, slope, part = call_rows(
            upper_kernel,
            rows,
            "upper",
            [tokens, part, twin(part)],
            [gains, shifts, bias_up.reshape(1, hidden), w_upper, w_lower],
            [(dim, F32), (128, F32), (dim, BF16), (hidden, BF16), (hidden, F32), (dim, BF16)],
            flops=2 * work,
        )
        out, grad_second, lower_grad, grad_upper, part, sums = call_rows(
            lower_kernel,
            rows,
            "lower",
            [normed1, part, twin(part), cotangent, slope],
            [gains, shifts, w_upper, w_lower],
            [(dim, BF16), (dim, F32), (dim, BF16), (hidden, BF16), (dim, BF16)],
            [hidden],
            flops=work,
        )
        other = twin(part)
        grad_low = dot(lower_grad.T, active).astype(BF16)
        grad_up = dot(first_low.T, grad_upper).astype(BF16)
        grad_first_sum, branch_grad, dout, deltat, small = call_rows(
            branch_kernel,
            rows,
            "branch",
            [grad_second, part, other, normed1, factor1, attended],
            [gains, sums, w_back],
            [(dim, F32), (dim, BF16), (width, BF16), (8, "turned")],
            [hidden],
            flops=work // 8,
        )
        stats = jnp.concatenate([lset, deltat], axis=0)
        got = send_rows(branch_grad, stats)
        small = jnp.pad(small, ((0, 0), (0, hidden + width)))
        grad_back = dot(branch_grad.T, attended).astype(BF16)
        group_a, small = send_f([grad_low, grad_up, grad_back], small)
        dq = query_grads(scalars, qkv, dout, stats, kb, rows, pairs)

        got = after(got, dq)
        stats_all = row_stats(stats, got, rows // 2)
        pieces, spots = row_pieces(branch_grad, got)
        (dout_all,) = project(scalars, pieces, spots, total, [w_back], None)
        group_a, small = finish_f(after(group_a, dq), small)
        state_a = send_1(group_a, small)
        dks, dvs = [], []
        gate = group_a
        for pair in range(pairs):
            dk, dv = key_grads(
                after(scalars, gate), qkv, dout_all, stats_all, kb, rows, pairs, pair
            )
            dks.append(dk)
            dvs.append(dv)
            gate = dk
            if pair == 0:
                state_a = finish_z(after(state_a, dk))
                gate = state_a
                state_a = send_2(*state_a)
            elif pair == 1:
                early = jnp.concatenate([dq] + dks + dvs, axis=1)
                row = jnp.sum(early.astype(F32), axis=0, keepdims=True)
                group_c, row = send_f([dot(tokens.T, early).astype(BF16)], row)
        late = jnp.concatenate([dks[-1], dvs[-1]], axis=1)
        tail = jnp.sum(late.astype(F32), axis=0, keepdims=True)
        group_d, tail = send_f([dot(tokens.T, late).astype(BF16)], tail)
        group_c, row = finish_f(after(group_c, late), row)
        state_a = send_3(*finish_z(after(state_a, late)))
        stacked = jnp.concatenate([dq] + dks + dvs, axis=1)
        input_part = pair_sum(dot(stacked, w_proj, ROW))
        grad_tokens = (grad_first_sum + input_part).astype(BF16)
        group_d, tail = finish_f(group_d, tail)
        both = jnp.concatenate([group_c, group_d], axis=1)
        row = jnp.concatenate([row, tail], axis=1)
        state_c = send_2(*finish_z(send_1(both, row)))
        group_a, small = finish_3(state_a)
        state_c = send_3(*finish_z(state_c))
        group_c, row = finish_3(state_c)

        sum_gains = jnp.stack([small[0, dim : 2 * dim], small[0, :dim]])
        sum_shifts = jnp.stack(
            [small[2, dim : 2 * dim], small[1, dim : 2 * dim], small[2, :dim], small[1, :dim]]
        )
        sum_bias_up = small[3, :hidden]
        low_k = 2 * width - 128
        low_v = low_k + width - 128
        sum_bias_qv = jnp.stack(
            [row[0, :width], jnp.concatenate([row[0, low_k:low_v], row[0, low_v + 128 :]])]
        )
        share_qkv = jnp.stack(
            [
                group_c[:, :width],
                jnp.concatenate([group_c[:, width:low_k], group_c[:, low_v : low_v + 128]], axis=1),
                jnp.concatenate([group_c[:, low_k:low_v], group_c[:, low_v + 128 :]], axis=1),
            ]
        )
        share_lower = group_a[:, :hidden].T
        share_upper = group_a[:, hidden : 2 * hidden]
        share_back = group_a[:, 2 * hidden :].T
        return (
            out,
            grad_tokens,
            share_qkv,
            share_back,
            share_upper,
            share_lower,
            sum_bias_qv,
            sum_bias_up,
            sum_gains,
            sum_shifts,
        )

    return jax.shard_map(
        shards,
        mesh=mesh,
        in_specs=(
            P(("fsdp", "context"), None),
            P(("fsdp", "context"), None),
            P(None, "fsdp", "tensor"),
            P(None, "tensor"),
            P("tensor", "fsdp"),
            P("fsdp", "tensor"),
            P("tensor"),
            P("tensor", "fsdp"),
            P(),
            P(),
            P("fsdp", None),
            P("fsdp"),
        ),
        out_specs=(
            P(("fsdp", "context"), None),
            P(("fsdp", "context"), None),
            P(None, "fsdp", "tensor"),
            P("tensor", "fsdp"),
            P("fsdp", "tensor"),
            P("tensor", "fsdp"),
            P(None, "tensor"),
            P("tensor"),
            P(),
            P(),
        ),
        check_vma=False,
    )
```
